128 devices in a mesh: tiles: 32 (over z, x, core), ens: 4 (over y).
Axes of the slice: x: 4, y: 4, z: 4, core: 2. Of those that a mesh axis runs over, the one named last changes fastest.
Arguments:
- depth: float32 [8, 512, 16384], P('ens', 'tiles'), may hold values from 0.3 to 1.5
- bed: float32 [512, 16384], P('tiles'), may hold values from -1.5 to 1.5
- rain: float32 [8, 512, 16384], P('ens', 'tiles'), may hold values from 0.005 to 0.05
- rough_class: int32 [512, 16384], P('tiles'), may hold values from 0 to 15
- class_n: float32 [16], replicated, may hold values from 0.5 to 2
- contact_seg: int32 [32, 32, 8], P('tiles'), may hold values from 0 to 1023, as said below
- contact_lake: int32 [32, 32, 8], P('tiles'), may hold values from -1 to 1279, as said below
- lake_slot: int32 [1280], replicated, may hold values from 0 to 1279, as said below
- storage: float32 [8, 1280], P('ens', 'tiles'), may hold values from 0.5 to 3
- area: float32 [1280], P('tiles'), may hold values from 1 to 4
- release: float32 [1280], P('tiles'), may hold values from 0.5 to 0.98
- upstream_link: int32 [1280], P('tiles'), may hold values from 0 to 1, as said below
Outputs:
- new_depth: float32 [8, 512, 16384], P('ens', 'tiles')
- new_storage: float32 [8, 1280], P('ens', 'tiles')
- ens_outflow: float32 [1280], P('tiles')
The draws below stay inside these ranges and needn't reach their ends.
Inputs may be any that keep to these rules, and one draw needn't show every extreme that they name: `contact_seg`: within one source tile the segments of all contact slots are distinct. `contact_lake`: A live entry [d, e, c] names a lake whose slot lake_slot lies on owner tile e (slots e * 40 onward); at most 8 live contacts go from one tile to one owner, and some owner receives 8 from every tile. `lake_slot`: A permutation of the slots. `upstream_link`: slots with index below 40 have 0; runs of linked slots form cascades of at most 16 reservoirs, and one cascade has exactly 16.
All inputs are finite; a program needn't handle non-finite values.
Results may differ from the reference program's by a relative error of at most 0.0001.
Values sent between devices are 32-bit elements; how exact they have to be, the bound alone decides.
A program may use at most 64 MiB of HBM per device.

```python
import math
import jax
import jax.numpy as jnp
from jax import lax

R_DEV = 16
W = 16384
SEG = 256
LAKE_DEV = 40
CAP = 8
NCLASS = 16
STEPS = 4
NY = 512
MEMB = 8
LAKES = 1280
DEPTH = 16
N_TILES = 32


def lake_order(key):
    return jax.random.permutation(jax.random.fold_in(key, 11), LAKES).astype(jnp.int32)


def draw_lake_slot(key, part):
    return lake_order(key)


def draw_contact_lake(key, part):
    shuffle = lake_order(key)
    slot_lake = jnp.argsort(shuffle, stable=True).astype(jnp.int32)
    key_count, key_hot, key_place = jax.random.split(jax.random.fold_in(key, 12), 3)
    counts = jax.random.randint(key_count, (N_TILES, N_TILES), 0, CAP + 1)
    hot_owner = jax.random.randint(key_hot, (2,), 0, N_TILES)
    owners = jnp.arange(N_TILES, dtype=jnp.int32)
    is_hot = jnp.any(owners[:, None] == hot_owner[None, :], axis=1)
    counts = jnp.where(is_hot[None, :], CAP, counts)
    position = jax.random.randint(key_place, (N_TILES, N_TILES, CAP), 0, LAKE_DEV)
    slot_id = owners[None, :, None] * LAKE_DEV + position
    live_mask = jnp.arange(CAP)[None, None, :] < counts[:, :, None]
    return jnp.where(live_mask, slot_lake[slot_id], -1).astype(jnp.int32)


def draw_contact_seg(key, part):
    wanted = N_TILES * CAP
    total_segs = R_DEV * (W // SEG)
    key_list = jax.random.split(jax.random.fold_in(key, 13), N_TILES)

    def one_device(device_key):
        key_first, key_second = jax.random.split(device_key)
        others = 1 + jax.random.permutation(key_first, total_segs - 2)[:wanted - 2]
        chosen = jnp.concatenate([jnp.array([0, total_segs - 1], jnp.int32), others.astype(jnp.int32)])
        return jax.random.permutation(key_second, chosen)
    return jax.vmap(one_device)(key_list).reshape(N_TILES, N_TILES, CAP).astype(jnp.int32)


def draw_upstream_link(key, part):
    key_length, key_offset = jax.random.split(jax.random.fold_in(key, 14))
    lengths = jax.random.randint(key_length, (LAKE_DEV,), 1, DEPTH + 1).at[0].set(DEPTH)
    offsets = (jax.random.randint(key_offset, (LAKE_DEV,), 0, DEPTH) % lengths).at[0].set(0)
    device_row = jnp.arange(N_TILES, dtype=jnp.int32)[:, None]
    linked = ((device_row - offsets[None, :]) % lengths[None, :] != 0) & (device_row > 0)
    return linked.astype(jnp.int32).reshape(-1)


def set_ends(entries, rng, least, top_value):
    longest = entries.shape.index(max(entries.shape))
    spots = []
    for shift in (0, 1):
        where = [jax.random.randint(jax.random.fold_in(rng, axis), (), 0, length) for axis, length in enumerate(entries.shape)]
        where[longest] = (where[longest] + shift) % entries.shape[longest]
        spots.append(tuple(where))
    return entries.at[spots[0]].set(least).at[spots[1]].set(top_value)


def shard_levels(rng, dims, cuts, least, top_value):
    def one(dim, blocks):
        steps = jax.random.uniform(jax.random.fold_in(jax.random.fold_in(rng, 6), dim), (blocks,), jnp.float32, least / len(cuts), top_value / len(cuts))
        return jnp.repeat(jnp.exp(steps), dims[dim] // blocks).reshape((-1,) + (1,) * (len(dims) - dim - 1))

    level = one(*cuts[0])
    for cut in cuts[1:]:
        level = level * one(*cut)
    return level


def centred(key, extent, spread, most, cuts=(), kind=jnp.bfloat16):
    loudness = shard_levels(key, extent, cuts, -0.22, 0.18) if cuts else 1.0
    result = jax.random.normal(key, extent, jnp.float32) * spread * loudness
    return jnp.minimum(jnp.maximum(result, -most), most).astype(kind)


def setup_inputs(seed: int = 0) -> dict:
    splits = jax.random.split(jax.random.key(seed), 13)
    depth = jnp.clip(0.3 + 1.2 * jax.random.uniform(splits[0], (MEMB, NY, W), jnp.float32) ** shard_levels(splits[0], (MEMB, NY, W), ((0, 4), (1, 32)), -0.2, 0.2), 0.3, 1.5)
    bed = centred(splits[1], (NY, W), 0.3, 1.5, ((0, 32),), jnp.float32)
    rain = jnp.clip(jnp.exp(math.log(0.05) - 2.3025851 * jax.random.uniform(splits[2], (MEMB, NY, W), jnp.float32) ** shard_levels(splits[2], (MEMB, NY, W), ((0, 4), (1, 32)), -0.2, 0.2)), 0.005, 0.05)
    rough_class = set_ends(jax.random.randint(splits[3], (NY, W), 0, NCLASS), jax.random.fold_in(splits[3], 1), 0, NCLASS - 1).astype(jnp.int32)
    class_n = jnp.clip(jnp.exp(jax.random.uniform(splits[4], (NCLASS,), jnp.float32, math.log(0.5), math.log(2.0))), 0.5, 2.0)
    contact_seg = draw_contact_seg(jax.random.fold_in(splits[12], 71), 0)
    contact_lake = draw_contact_lake(jax.random.fold_in(splits[12], 71), 0)
    lake_slot = draw_lake_slot(jax.random.fold_in(splits[12], 71), 0)
    storage = jnp.clip(0.5 + 2.5 * jax.random.uniform(splits[8], (MEMB, LAKES), jnp.float32) ** shard_levels(splits[8], (MEMB, LAKES), ((0, 4), (1, 32)), -0.2, 0.2), 0.5, 3.0)
    area = jnp.clip(jnp.exp(math.log(4.0) - 1.3862944 * jax.random.uniform(splits[9], (LAKES,), jnp.float32) ** shard_levels(splits[9], (LAKES,), ((0, 32),), -0.2, 0.2)), 1.0, 4.0)
    release = jnp.clip(0.5 + 0.48000002 * jax.random.uniform(splits[10], (LAKES,), jnp.float32) ** shard_levels(splits[10], (LAKES,), ((0, 32),), -0.2, 0.2), 0.5, 0.98)
    upstream_link = draw_upstream_link(jax.random.fold_in(splits[12], 71), 0)
    return dict(depth=depth, bed=bed, rain=rain, rough_class=rough_class, class_n=class_n, contact_seg=contact_seg, contact_lake=contact_lake, lake_slot=lake_slot, storage=storage, area=area, release=release, upstream_link=upstream_link)


flow_rate = 0.035
drain_rate = 0.4


def mobility(water, inv_n):
    root = jnp.cbrt(water)
    return water * root * root * inv_n


def surface_flow(water, bed, inv_n):
    surface = bed[None] + water
    mobile = mobility(water, inv_n[None])
    pad_surface = jnp.pad(surface, ((0, 0), (1, 1), (0, 0)))
    pad_mobile = jnp.pad(mobile, ((0, 0), (1, 1), (0, 0)))
    face_count = surface.shape[1] + 1
    face_index = jnp.arange(face_count)
    face_mask = ((face_index > 0) & (face_index < face_count - 1)).astype(water.dtype)[None, :, None]
    across = face_mask * 0.5 * (pad_mobile[:, :-1] + pad_mobile[:, 1:]) * (pad_surface[:, :-1] - pad_surface[:, 1:])
    sideways = 0.5 * (mobile[..., :-1] + mobile[..., 1:]) * (surface[..., :-1] - surface[..., 1:])
    zero_col = jnp.zeros(water.shape[:2] + (1,), water.dtype)
    inflow_net = across[:, :-1] - across[:, 1:] + jnp.concatenate([zero_col, sideways], -1) - jnp.concatenate([sideways, zero_col], -1)
    return water + flow_rate * inflow_net


def reference(depth, bed, rain, rough_class, class_n, contact_seg, contact_lake, lake_slot, storage, area, release, upstream_link):
    classes = jnp.arange(NCLASS, dtype=jnp.int32)
    inv_n = jnp.sum(jnp.where(rough_class[None] == classes[:, None, None], (1.0 / class_n)[:, None, None], 0.0), axis=0)
    per_row = W // SEG
    segs_dev = R_DEV * per_row
    source = jnp.arange(N_TILES, dtype=jnp.int32)[:, None, None]
    global_seg = (contact_seg + source * segs_dev).reshape(-1).astype(jnp.int32)
    lake_ids = contact_lake.reshape(-1)
    live_mask = lake_ids >= 0
    slots = jnp.where(live_mask, lake_slot[jnp.maximum(lake_ids, 0)], 0).astype(jnp.int32)
    live_float = live_mask.astype(storage.dtype)[None, :, None]
    linked = upstream_link.astype(storage.dtype)
    scale_a = (release * linked).reshape(N_TILES, LAKE_DEV)
    water = depth
    pool_store = storage
    outflow_sum = jnp.zeros_like(storage)
    for routing_step in range(STEPS):
        wetted = surface_flow(water, bed, inv_n) + rain
        pool_level = pool_store / area[None]
        wet_seg = wetted.reshape(MEMB, NY * per_row, SEG)
        bed_seg = bed.reshape(NY * per_row, SEG)
        wet_contact = wet_seg[:, global_seg]
        surf_contact = bed_seg[global_seg][None] + wet_contact
        excess = jnp.maximum(surf_contact - pool_level[:, slots][..., None], 0.0)
        taken_water = drain_rate * wet_contact * excess / (1.0 + excess) * live_float
        water = wet_seg.at[:, global_seg].add(-taken_water).reshape(MEMB, NY, W)
        slot_sums = jnp.sum(taken_water, axis=-1)
        lateral = jax.ops.segment_sum(slot_sums.T, slots, num_segments=LAKES).T / SEG
        scale_b = (release[None] * (pool_store + lateral)).reshape(MEMB, N_TILES, LAKE_DEV).transpose(1, 0, 2)

        def link_step(carried, inputs):
            factor, offset = inputs
            released_now = factor * carried + offset
            return released_now, (released_now, carried)

        start = jnp.zeros((MEMB, LAKE_DEV), storage.dtype)
        unused, (released_blocks, above_blocks) = lax.scan(link_step, start, (scale_a[:, None, :], scale_b))
        released = released_blocks.transpose(1, 0, 2).reshape(MEMB, LAKES)
        from_above = above_blocks.transpose(1, 0, 2).reshape(MEMB, LAKES)
        pool_store = pool_store + lateral + linked[None] * from_above - released
        outflow_sum = outflow_sum + released
    ens_outflow = jnp.sum(outflow_sum, axis=0) / MEMB
    return water, pool_store, ens_outflow
```

```python
import jax
import jax.numpy as jnp
from jax import lax
from jax.experimental import pallas as pl
from jax.experimental.pallas import tpu as pltpu
from jax.sharding import PartitionSpec as P

STEPS = 4
TILES = 32
ENS = 4
MEMB = 2
ROWS = 16
COLS = 16384
BLOCKS = 16
LAKE_DEV = 40
FLOW = 0.035
DRAIN = 0.4
FAR = 3.0e38
MESH = pl.DeviceIdType.MESH
F32 = jnp.float32
I32 = jnp.int32


def iota(axis):
    return lax.broadcasted_iota(I32, (8, 128), axis)


def merge(a, b, index, bit, axis):
    odd = (index & bit) != 0
    return jnp.where(odd, b, a) + pltpu.roll(jnp.where(odd, a, b), bit, axis)


def spread(row):
    return jnp.broadcast_to(row, (8, 128))


def lanes_of(table, index):
    return jnp.take_along_axis(table, index, axis=1)


def power(water):
    return water * jnp.exp2(jnp.log2(jnp.abs(water)) * (2.0 / 3.0))


def peer_offsets():
    near = {0: 0, 1: 1, 2: 2, 3: 1}
    found = [
        (z, x, c) for z in range(4) for x in range(4) for c in range(2) if (z, x, c) != (0, 0, 0)
    ]
    return sorted(found, key=lambda o: (-near[o[0]] - near[o[1]], o))


def kernel(
    depth, bed_in, rain_in, rough, class_n, contact_seg, contact_lake, lake_slot,
    storage, area, release, link,
    new_depth, new_storage, ens_outflow,
    wat, rain, bed, ivn, wet, rgh,
    seg_s, lake_s, slot_s, cls_v, sto_v, are_v, rel_v, lnk_v,
    hello, greet, turn, pos, pool, outf, par,
    edge0, halo0, edge, halo, flux, part, msg, got, emsg, egot,
    lsem, psem, isem, ssem, rsem, hsend, hrecv, esend, erecv, osem,
):
    me = lax.axis_index("tiles")
    ye = lax.axis_index("ens")
    sub, lane = iota(0), iota(1)
    before, after = lax.rem(me + TILES - 1, TILES), lax.rem(me + 1, TILES)
    z, x, core = me // 8, (me // 2) % 4, me % 2
    peers = [
        (lax.rem(z + dz, 4) * 4 + lax.rem(x + dx, 4)) * 2 + lax.rem(core + dc, 2)
        for dz, dx, dc in peer_offsets()
    ]
    others = [lax.rem(ye + k, ENS) for k in range(1, ENS)]

    smalls = [
        (contact_seg, seg_s), (contact_lake, lake_s), (lake_slot, slot_s), (class_n, cls_v),
        (storage, sto_v), (area, are_v), (release, rel_v), (link, lnk_v),
    ]
    bigs = [(rough, rgh), (bed_in, bed), (depth, wat), (rain_in, rain)]
    loads = [pltpu.make_async_copy(a, b, lsem.at[i]) for i, (a, b) in enumerate(smalls + bigs)]
    for load in loads:
        load.start()

    barrier = pltpu.get_barrier_semaphore()
    for peer in peers:
        pl.semaphore_signal(barrier, inc=1, device_id={"tiles": peer}, device_id_type=MESH)
    for other in others:
        pl.semaphore_signal(barrier, inc=1, device_id={"ens": other}, device_id_type=MESH)

    for load in loads[: len(smalls)]:
        load.wait()

    seg_id = ((lane & 1) * 8 + sub) * 64 + (lane >> 1)
    contact_id = (lane & 31) * 8 + (sub >> 1) * 4 + (lane >> 5)

    def read_contacts(e, carry):
        code, from_seg, where_to = carry
        for c in range(8):
            seg = seg_s[0, e, c]
            lake = lake_s[0, e, c]
            live = lake >= 0
            place = slot_s[0, jnp.maximum(lake, 0)] - e * LAKE_DEV
            code = jnp.where(seg_id == seg, jnp.where(live, place * 32 + e, -1), code)
            mine = contact_id == e * 8 + c
            from_seg = jnp.where(mine, seg, from_seg)
            where_to = jnp.where(mine, jnp.where(live, place, -1), where_to)
        return code, from_seg, where_to

    none = jnp.full((8, 128), -1, I32)
    code, from_seg, where_to = lax.fori_loop(
        0, TILES, read_contacts, (none, jnp.zeros((8, 128), I32), none)
    )
    code_row, code_lane = code >> 7, code & 127
    src_sub = (from_seg >> 6) & 7
    src_lane = (from_seg & 63) * 2 + (from_seg >> 9)

    place_rows = where_to.astype(F32)
    hello[...] = jnp.zeros((8, 128), F32)
    hello[0:1, :] = place_rows[0:1, :]
    hello[1:2, :] = place_rows[2:3, :]
    hello[2:4, 0:LAKE_DEV] = sto_v[...]
    hello[4:5, 0:LAKE_DEV] = are_v[...]
    hello[5:6, 0:LAKE_DEV] = rel_v[...]
    hello[6:7, 0:LAKE_DEV] = lnk_v[...].astype(F32)

    pl.semaphore_wait(barrier, TILES - 1 + ENS - 1)
    for peer in peers:
        pltpu.make_async_remote_copy(
            hello, greet.at[me], psem, isem, device_id={"tiles": peer}, device_id_type=MESH
        ).start()
    pltpu.make_async_copy(hello, greet.at[me], isem).start()

    for load in loads[len(smalls):]:
        load.wait()
    inverse = (0.5 * FLOW) / cls_v[...]
    turn[...] = jnp.zeros((128, 128), F32)
    turn[0:1, 0:16] = inverse
    classes = spread(turn[0:1, :])

    def read_rough(i, carry):
        base = pl.multiple_of(i * 1024, 1024)
        for j in range(8):
            cols = pl.ds(base + j * 128, 128)
            for half in range(2):
                rows = slice(half * 8, half * 8 + 8)
                ivn[rows, cols] = lanes_of(classes, rgh[rows, cols])
            for side, row in ((0, 0), (1, 15)):
                edge0[side, 0, i, j:j + 1, :] = wat[0, row:row + 1, cols]
                edge0[side, 1, i, j:j + 1, :] = wat[1, row:row + 1, cols]
                edge0[side, 2, i, j:j + 1, :] = bed[row:row + 1, cols]
                edge0[side, 3, i, j:j + 1, :] = ivn[row:row + 1, cols]
        return carry

    lax.fori_loop(0, BLOCKS, read_rough, 0)

    def halo_copies(step):
        source, target = (edge0, halo0) if step == 0 else (edge.at[step - 1], halo.at[step - 1])
        return [
            pltpu.make_async_remote_copy(
                source.at[side], target.at[1 - side], hsend.at[step, side], hrecv.at[step, side],
                device_id={"tiles": (before, after)[side]}, device_id_type=MESH,
            )
            for side in (0, 1)
        ]

    def flows(step):
        mine, theirs = (edge0, halo0) if step == 0 else (edge.at[step - 1], halo.at[step - 1])
        inside = (me > 0, me < TILES - 1)

        def edge_flux(i, carry):
            for side in (0, 1):
                for m in range(MEMB):
                    w_own, w_far = mine[side, m, i], theirs[side, m, i]
                    s_own = w_own + edge0[side, 2, i]
                    s_far = w_far + halo0[side, 2, i]
                    m_own = power(w_own) * edge0[side, 3, i]
                    m_far = power(w_far) * halo0[side, 3, i]
                    value = (m_own + m_far) * ((s_far - s_own) if side == 0 else (s_own - s_far))
                    flux[side, m, i] = jnp.where(inside[side], value, 0.0)
            return carry

        lax.fori_loop(0, BLOCKS, edge_flux, 0)
        top, bottom = sub == 0, sub == 7
        first, last = lane == 0, lane == 127

        def block(i, carry):
            carry = list(carry)
            base = pl.multiple_of(i * 1024, 1024)
            for j in range(8):
                cols = pl.ds(base + j * 128, 128)
                done = pl.ds(base + j * 128, 128)
                beds = [bed[h * 8:h * 8 + 8, cols] for h in range(2)]
                invs = [ivn[h * 8:h * 8 + 8, cols] for h in range(2)]
                for m in range(MEMB):
                    w = [wat[m, h * 8:h * 8 + 8, cols] for h in range(2)]
                    s = [beds[h] + w[h] for h in range(2)]
                    mo = [power(w[h]) * invs[h] for h in range(2)]
                    s_dn = [pltpu.roll(v, 1, 0) for v in s]
                    m_dn = [pltpu.roll(v, 1, 0) for v in mo]
                    fv0 = jnp.where(
                        top, spread(flux[0, m, i, j:j + 1, :]), (m_dn[0] + mo[0]) * (s_dn[0] - s[0])
                    )
                    fv1 = (jnp.where(top, m_dn[0], m_dn[1]) + mo[1]) * (
                        jnp.where(top, s_dn[0], s_dn[1]) - s[1]
                    )
                    up0, up1 = pltpu.roll(fv0, 7, 0), pltpu.roll(fv1, 7, 0)
                    nv = [
                        fv0 - jnp.where(bottom, up1, up0),
                        fv1 - jnp.where(bottom, spread(flux[1, m, i, j:j + 1, :]), up1),
                    ]
                    for h in range(2):
                        at = (m * 2 + h) * 4
                        s_prev, m_prev, f_prev, sum_prev = carry[at:at + 4]
                        s_rt, m_rt = pltpu.roll(s[h], 1, 1), pltpu.roll(mo[h], 1, 1)
                        f = (jnp.where(first, m_prev, m_rt) + mo[h]) * (
                            jnp.where(first, s_prev, s_rt) - s[h]
                        )
                        f_lt = pltpu.roll(f, 127, 1)
                        wet[m, h * 8:h * 8 + 8, done] = sum_prev - jnp.where(last, f_lt, f_prev)
                        total = (w[h] + rain[m, h * 8:h * 8 + 8, cols]) + (nv[h] + f)
                        carry[at:at + 4] = [s_rt, m_rt, f_lt, total]
            return tuple(carry)

        zero = jnp.zeros((8, 128), F32)
        start = []
        for m in range(MEMB):
            for h in range(2):
                rows = slice(h * 8, h * 8 + 8)
                start += [bed[rows, 0:128] + wat[m, rows, 0:128], zero, zero, zero]
        carry = lax.fori_loop(0, BLOCKS, block, tuple(start))
        for m in range(MEMB):
            for h in range(2):
                f_prev, sum_prev = carry[(m * 2 + h) * 4 + 2:(m * 2 + h) * 4 + 4]
                wet[m, h * 8:h * 8 + 8, COLS:COLS + 128] = sum_prev - jnp.where(last, 0.0, f_prev)

    def drain(step, levels):
        found = [jnp.full((8, 128), FAR, F32) for _ in range(MEMB)]
        for j in range(LAKE_DEV // 4):
            here = code_row == j
            for m in range(MEMB):
                r = 2 * j + m
                row = spread(levels[r // 8][r % 8:r % 8 + 1, :])
                found[m] = jnp.where(here, lanes_of(row, code_lane), found[m])

        def block(i, carry):
            base = pl.multiple_of(i * 1024, 1024)
            shift = lax.rem(128 - i * 8, 128)
            beds = {}
            for m in range(MEMB):
                turned = pltpu.roll(found[m], shift, 1)
                leaves = []
                for g in range(4):
                    for h in range(2):
                        rows = slice(h * 8, h * 8 + 8)
                        level = spread(turned[:, 2 * g + h:2 * g + h + 1])
                        leaf = None
                        for j in (2 * g, 2 * g + 1):
                            cols = pl.ds(base + j * 128, 128)
                            w = wet[m, rows, pl.ds(base + j * 128 + 128, 128)]
                            excess = jnp.maximum((bed[rows, cols] + w) - level, 0.0)
                            taken = (DRAIN * w) * (excess / (1.0 + excess))
                            left = w - taken
                            wat[m, rows, cols] = left
                            if step < STEPS - 1:
                                r = 0 if h == 0 else 7
                                edge[step, h, m, i, j:j + 1, :] = left[r:r + 1, :]
                            leaf = taken if leaf is None else leaf + taken
                        leaves.append(leaf)
                for bit in (1, 2, 4):
                    leaves = [
                        merge(leaves[n], leaves[n + 1], lane, bit, 1)
                        for n in range(0, len(leaves), 2)
                    ]
                part[m, i] = leaves[0]
            return carry

        lax.fori_loop(0, BLOCKS, block, 0)
        sums = []
        for m in range(MEMB):
            leaves = [part[m, i] for i in range(BLOCKS)]
            for bit in (8, 16, 32, 64):
                leaves = [
                    merge(leaves[n], leaves[n + 1], lane, bit, 1) for n in range(0, len(leaves), 2)
                ]
            sums.append(leaves[0])
        return sums

    def tell(step, sums):
        picked = [jnp.zeros((8, 128), F32) for _ in range(MEMB)]
        for k in range(8):
            here = src_sub == k
            for m in range(MEMB):
                row = spread(sums[m][k:k + 1, :])
                picked[m] = jnp.where(here, lanes_of(row, src_lane), picked[m])
        msg[step] = jnp.where((sub & 1) == 0, picked[0], picked[1])[0:4, :]
        for peer in peers:
            pltpu.make_async_remote_copy(
                msg.at[step], got.at[step, me], ssem.at[step], rsem.at[step],
                device_id={"tiles": peer}, device_id_type=MESH,
            ).start()
        pltpu.make_async_copy(msg.at[step], got.at[step, me], rsem.at[step]).start()

    def hear(step):
        pltpu.make_async_copy(got.at[step], got.at[step], rsem.at[step]).wait()
        values = [
            jnp.concatenate([got[step, 2 * n], got[step, 2 * n + 1]], axis=0)
            for n in range(TILES // 2)
        ]
        places = [pos[n] for n in range(TILES // 2)]
        lateral = []
        for v in range(3):
            leaves = []
            for p in range(v * 16, min(v * 16 + 16, LAKE_DEV)):
                terms = [
                    jnp.where(places[n] == float(p), values[n], 0.0) for n in range(TILES // 2)
                ]
                while len(terms) > 1:
                    terms = [terms[n] + terms[n + 1] for n in range(0, len(terms), 2)]
                leaves.append(terms[0])
            for index, bit, axis in ((lane, 32, 1), (lane, 64, 1), (sub, 2, 0)):
                leaves = [
                    merge(leaves[n], leaves[n + 1], index, bit, axis)
                    for n in range(0, len(leaves), 2)
                ]
            if len(leaves) == 1:
                leaves.append(jnp.zeros((8, 128), F32))
            lateral.append(merge(leaves[0], leaves[1], sub, 4, 0) * (1.0 / 256.0))
        for v in range(3):
            rows = slice(v * 8, v * 8 + 8)
            held = pool[rows, :]
            out = par[1, rows, :] * (held + lateral[v])
            for stage, shift in ((3, 1), (4, 2), (5, 4), (6, 8)):
                out = out + par[stage, rows, :] * pltpu.roll(out, shift, 1)
            above = par[2, rows, :] * pltpu.roll(out, 1, 1)
            pool[rows, :] = held + lateral[v] + above - out
            outf[rows, :] = outf[rows, :] + out

    def level_now():
        return [pool[v * 8:v * 8 + 8, :] * par[0, v * 8:v * 8 + 8, :] for v in range(3)]

    for copy in halo_copies(0):
        copy.start()

    pltpu.make_async_copy(greet, greet, isem).wait()
    for n in range(TILES // 2):
        quarter = [
            spread(greet[2 * n + d, c:c + 1, :]) for d in range(2) for c in range(2)
        ]
        pos[n] = jnp.where(
            sub < 4,
            jnp.where(sub < 2, quarter[0], quarter[1]),
            jnp.where(sub < 6, quarter[2], quarter[3]),
        )
    for k in range(4):
        pick = (lane & 15) * 4 + k
        for b in range(4):
            tile = jnp.zeros((8, 128), F32)
            for kind in range(5):
                rows = greet[b * 8:b * 8 + 8, 2 + kind, :]
                tile = jnp.where((lane >> 4) == kind, lanes_of(rows, pick), tile)
            turn[k * 32 + b * 8:k * 32 + b * 8 + 8, :] = tile
    turn[...] = jnp.transpose(turn[...])
    pool[...] = jnp.zeros((24, 128), F32)
    outf[...] = jnp.zeros((24, 128), F32)
    par[0] = jnp.ones((24, 128), F32)
    par[1] = jnp.zeros((24, 128), F32)
    par[2] = jnp.zeros((24, 128), F32)
    for j in range(LAKE_DEV // 4):
        for m in range(MEMB):
            r = 2 * j + m
            pool[r:r + 1, :] = turn[16 * m + j:16 * m + j + 1, :]
            for kind in range(3):
                at = 32 + 16 * kind + j
                par[kind, r:r + 1, :] = turn[at:at + 1, :]
    for v in range(3):
        rows = slice(v * 8, v * 8 + 8)
        par[0, rows, :] = 1.0 / par[0, rows, :]
        chain = par[1, rows, :] * par[2, rows, :]
        for stage, shift in ((3, 1), (4, 2), (5, 4), (6, 8)):
            par[stage, rows, :] = chain
            chain = chain * pltpu.roll(chain, shift, 1)

    for step in range(STEPS):
        for copy in halo_copies(step):
            copy.wait_recv()
        flows(step)
        if step > 0:
            hear(step - 1)
        sums = drain(step, level_now())
        tell(step, sums)
        if step < STEPS - 1:
            for copy in halo_copies(step + 1):
                copy.start()
    store = pltpu.make_async_copy(wat, new_depth, osem)
    store.start()
    hear(STEPS - 1)

    pick = (lane & 3) * 32 + me
    own = [jnp.zeros((8, 128), F32) for _ in range(2)]
    for j in range(LAKE_DEV // 4):
        for m in range(MEMB):
            r = 2 * j + m
            here = (lane >> 2) == j
            own[0] = jnp.where(
                here & ((sub & 1) == m), lanes_of(spread(pool[r:r + 1, :]), pick), own[0]
            )
            own[1] = own[1] + jnp.where(here, lanes_of(spread(outf[r:r + 1, :]), pick), 0.0)
    emsg[...] = own[1]
    for k, other in enumerate(others):
        pltpu.make_async_remote_copy(
            emsg, egot.at[ye], esend, erecv, device_id={"ens": other}, device_id_type=MESH
        ).start()
    pltpu.make_async_copy(emsg, egot.at[ye], erecv).start()
    new_storage[...] = own[0][0:2, 0:LAKE_DEV]
    pltpu.make_async_copy(egot, egot, erecv).wait()
    total = (egot[0] + egot[1] + egot[2] + egot[3]) * (1.0 / (MEMB * ENS))
    ens_outflow[...] = total[0:1, 0:LAKE_DEV]

    store.wait()
    pltpu.make_async_copy(greet.at[1:], greet.at[1:], psem).wait()
    for step in range(STEPS):
        for copy in halo_copies(step):
            copy.wait_send()
        pltpu.make_async_copy(got.at[step, 1:], got.at[step, 1:], ssem.at[step]).wait()
    pltpu.make_async_copy(egot.at[1:], egot.at[1:], esend).wait()


def shards(
    depth, bed, rain, rough_class, class_n, contact_seg, contact_lake, lake_slot,
    storage, area, release, upstream_link,
):
    anywhere = pl.BlockSpec(memory_space=pl.ANY)
    vmem = pl.BlockSpec(memory_space=pltpu.VMEM)
    dma = pltpu.SemaphoreType.DMA
    water, pool, outflow = pl.pallas_call(
        kernel,
        out_shape=(
            jax.ShapeDtypeStruct((MEMB, ROWS, COLS), F32),
            jax.ShapeDtypeStruct((MEMB, LAKE_DEV), F32),
            jax.ShapeDtypeStruct((1, LAKE_DEV), F32),
        ),
        in_specs=[anywhere] * 12,
        out_specs=(anywhere, vmem, vmem),
        scratch_shapes=[
            pltpu.VMEM((MEMB, ROWS, COLS), F32),
            pltpu.VMEM((MEMB, ROWS, COLS), F32),
            pltpu.VMEM((ROWS, COLS), F32),
            pltpu.VMEM((ROWS, COLS), F32),
            pltpu.VMEM((MEMB, ROWS, COLS + 128), F32),
            pltpu.VMEM((ROWS, COLS), I32),
            pltpu.SMEM((1, TILES, 8), I32),
            pltpu.SMEM((1, TILES, 8), I32),
            pltpu.SMEM((1, TILES * LAKE_DEV), I32),
            pltpu.VMEM((1, 16), F32),
            pltpu.VMEM((MEMB, LAKE_DEV), F32),
            pltpu.VMEM((1, LAKE_DEV), F32),
            pltpu.VMEM((1, LAKE_DEV), F32),
            pltpu.VMEM((1, LAKE_DEV), I32),
            pltpu.VMEM((8, 128), F32),
            pltpu.VMEM((TILES, 8, 128), F32),
            pltpu.VMEM((128, 128), F32),
            pltpu.VMEM((TILES // 2, 8, 128), F32),
            pltpu.VMEM((24, 128), F32),
            pltpu.VMEM((24, 128), F32),
            pltpu.VMEM((7, 24, 128), F32),
            pltpu.VMEM((2, 4, BLOCKS, 8, 128), F32),
            pltpu.VMEM((2, 4, BLOCKS, 8, 128), F32),
            pltpu.VMEM((STEPS - 1, 2, MEMB, BLOCKS, 8, 128), F32),
            pltpu.VMEM((STEPS - 1, 2, MEMB, BLOCKS, 8, 128), F32),
            pltpu.VMEM((2, MEMB, BLOCKS, 8, 128), F32),
            pltpu.VMEM((MEMB, BLOCKS, 8, 128), F32),
            pltpu.VMEM((STEPS, 4, 128), F32),
            pltpu.VMEM((STEPS, TILES, 4, 128), F32),
            pltpu.VMEM((8, 128), F32),
            pltpu.VMEM((ENS, 8, 128), F32),
            dma((12,)),
            dma,
            dma,
            dma((STEPS,)),
            dma((STEPS,)),
            dma((STEPS, 2)),
            dma((STEPS, 2)),
            dma,
            dma,
            dma,
        ],
        compiler_params=pltpu.CompilerParams(
            collective_id=0, has_side_effects=True, vmem_limit_bytes=40 * 1024 * 1024
        ),
    )(
        depth, bed, rain, rough_class, class_n.reshape(1, -1), contact_seg, contact_lake,
        lake_slot.reshape(1, -1), storage, area.reshape(1, -1), release.reshape(1, -1),
        upstream_link.reshape(1, -1),
    )
    return water, pool, outflow.reshape(-1)


def solution(mesh):
    return jax.shard_map(
        shards,
        mesh=mesh,
        in_specs=(
            P("ens", "tiles", None),
            P("tiles", None),
            P("ens", "tiles", None),
            P("tiles", None),
            P(),
            P("tiles", None, None),
            P("tiles", None, None),
            P(),
            P("ens", "tiles"),
            P("tiles"),
            P("tiles"),
            P("tiles"),
        ),
        out_specs=(P("ens", "tiles", None), P("ens", "tiles"), P("tiles")),
        check_vma=False,
    )
```

```python
import jax
import jax.numpy as jnp
from jax import lax
from jax.experimental import pallas as pl
from jax.experimental.pallas import tpu as pltpu
from jax.sharding import PartitionSpec as P

STEPS = 4
TILES = 32
ENS = 4
MEMB = 2
ROWS = 16
COLS = 16384
BLOCKS = 16
PARTS = 2
CHUNKS = 16
DEPTH = 16
SPAN = BLOCKS // PARTS
LAKE_DEV = 40
FLOW = 0.035
DRAIN = 0.4
FAR = 3.0e38
MESH = pl.DeviceIdType.MESH
F32 = jnp.float32
I32 = jnp.int32


def iota(axis):
    return lax.broadcasted_iota(I32, (8, 128), axis)


def merge(a, b, index, bit, axis):
    odd = (index & bit) != 0
    return jnp.where(odd, b, a) + pltpu.roll(jnp.where(odd, a, b), bit, axis)


def total_of(terms):
    while len(terms) > 1:
        pairs = [terms[n] + terms[n + 1] for n in range(0, len(terms) - 1, 2)]
        terms = pairs + ([terms[-1]] if len(terms) % 2 else [])
    return terms[0]


def spread(row):
    return jnp.broadcast_to(row, (8, 128))


def lanes_of(table, index):
    return jnp.take_along_axis(table, index, axis=1)


def power(water):
    return water * jnp.exp2(jnp.log2(jnp.abs(water)) * (2.0 / 3.0))


def peer_offsets():
    near = {0: 0, 1: 1, 2: 2, 3: 1}
    found = [
        (z, x, c) for z in range(4) for x in range(4) for c in range(2) if (z, x, c) != (0, 0, 0)
    ]
    return sorted(found, key=lambda o: (-near[o[0]] - near[o[1]], o))


def kernel(
    depth, bed_in, rain_in, rough, class_n, contact_seg, contact_lake, lake_slot,
    storage, area, release, link,
    water, new_storage, ens_outflow,
    wat, rain, bed, ivn, wet, rgh,
    seg_s, lake_s, slot_s, cls_v, sto_v, are_v, rel_v, lnk_v,
    hello, greet, turn, pos, pool, outf, par, chain,
    still, still_far, edge, halo, flux, level, part, lines, msg, got, emsg, egot,
    lsem, psem, isem, ssem, rsem, hsend, hrecv, bsend, brecv, esend, erecv,
):
    me = lax.axis_index("tiles")
    ye = lax.axis_index("ens")
    sub, lane = iota(0), iota(1)
    before, after = lax.rem(me + TILES - 1, TILES), lax.rem(me + 1, TILES)
    z, x, core = me // 8, (me // 2) % 4, me % 2
    peers = [
        (lax.rem(z + dz, 4) * 4 + lax.rem(x + dx, 4)) * 2 + lax.rem(core + dc, 2)
        for dz, dx, dc in peer_offsets()
    ]
    others = [lax.rem(ye + k, ENS) for k in range(1, ENS)]

    smalls = [
        (contact_seg, seg_s), (contact_lake, lake_s), (lake_slot, slot_s), (class_n, cls_v),
        (storage, sto_v), (area, are_v), (release, rel_v), (link, lnk_v),
    ]
    bigs = [(rough, rgh), (bed_in, bed), (depth, wat), (rain_in, rain)]
    loads = [pltpu.make_async_copy(a, b, lsem.at[i]) for i, (a, b) in enumerate(smalls + bigs)]
    for load in loads:
        load.start()

    barrier = pltpu.get_barrier_semaphore()
    for peer in peers:
        pl.semaphore_signal(barrier, inc=1, device_id={"tiles": peer}, device_id_type=MESH)
    for other in others:
        pl.semaphore_signal(barrier, inc=1, device_id={"ens": other}, device_id_type=MESH)

    for load in loads[: len(smalls)]:
        load.wait()

    seg_id = ((lane & 1) * 8 + sub) * 64 + (lane >> 1)
    contact_id = (lane & 31) * 8 + sub * 4 + (lane >> 5)

    def read_contacts(e, carry):
        code, from_seg, where_to = carry
        for c in range(8):
            seg = seg_s[0, c, e]
            lake = lake_s[0, c, e]
            live = lake >= 0
            place = slot_s[jnp.maximum(lake, 0)] - e * LAKE_DEV
            code = jnp.where(seg_id == seg, jnp.where(live, place * 32 + e, -1), code)
            mine = (contact_id == e * 8 + c) & (sub < 2)
            from_seg = jnp.where(mine, seg, from_seg)
            where_to = jnp.where(mine, jnp.where(live, place, -1), where_to)
        return code, from_seg, where_to

    none = jnp.full((8, 128), -1, I32)
    code, from_seg, where_to = lax.fori_loop(
        0, TILES, read_contacts, (none, jnp.zeros((8, 128), I32), none)
    )
    code_row, code_lane = code >> 7, code & 127
    src_sub = (from_seg >> 6) & 7
    src_lane = (from_seg & 63) * 2 + (from_seg >> 9)

    hello[...] = jnp.zeros((8, 128), F32)
    hello[0:2, :] = where_to.astype(F32)[0:2, :]
    hello[2:4, 0:LAKE_DEV] = sto_v[...]
    hello[4:5, 0:LAKE_DEV] = are_v[...]
    hello[5:6, 0:LAKE_DEV] = rel_v[...]
    hello[6:7, 0:LAKE_DEV] = lnk_v[...].astype(F32)

    pl.semaphore_wait(barrier, TILES - 1 + ENS - 1)
    for peer in peers:
        pltpu.make_async_remote_copy(
            hello, greet.at[me], psem, isem, device_id={"tiles": peer}, device_id_type=MESH
        ).start()
    pltpu.make_async_copy(hello, greet.at[me], isem).start()

    for load in loads[len(smalls):]:
        load.wait()
    inverse = (0.5 * FLOW) / cls_v[...]
    classes = [spread(inverse[:, n:n + 1]) for n in range(16)]

    def inverse_of(index):
        found = classes
        for bit in (1, 2, 4, 8):
            odd = (index & bit) != 0
            found = [jnp.where(odd, found[n + 1], found[n]) for n in range(0, len(found), 2)]
        return found[0]

    def read_rough(i, carry):
        base = pl.multiple_of(i * 1024, 1024)
        for j in range(8):
            cols = pl.ds(base + j * 128, 128)
            for half in range(2):
                rows = slice(half * 8, half * 8 + 8)
                ivn[rows, cols] = inverse_of(rgh[rows, cols])
            for side, row in ((0, 0), (1, 15)):
                edge[0, side, 0, i, j:j + 1, :] = wat[0, row:row + 1, cols]
                edge[0, side, 1, i, j:j + 1, :] = wat[1, row:row + 1, cols]
                still[side, 0, i, j:j + 1, :] = bed[row:row + 1, cols]
                still[side, 1, i, j:j + 1, :] = ivn[row:row + 1, cols]
        return carry

    lax.fori_loop(0, BLOCKS, read_rough, 0)

    def beside(side):
        return {"tiles": (before, after)[side]}

    still_copies = [
        pltpu.make_async_remote_copy(
            still.at[side], still_far.at[1 - side], bsend.at[side], brecv.at[side],
            device_id=beside(side), device_id_type=MESH,
        )
        for side in (0, 1)
    ]

    def halo_copies(step, p):
        at = pl.ds(p * SPAN, SPAN)
        return [
            pltpu.make_async_remote_copy(
                edge.at[step, side, :, at], halo.at[step, 1 - side, :, at],
                hsend.at[step, side, p], hrecv.at[step, side, p],
                device_id=beside(side), device_id_type=MESH,
            )
            for side in (0, 1)
        ]

    def edge_flows(step):
        inside = (me > 0, me < TILES - 1)

        def edge_flux(i, carry):
            for side in (0, 1):
                for m in range(MEMB):
                    w_own, w_far = edge[step, side, m, i], halo[step, side, m, i]
                    s_own, s_far = w_own + still[side, 0, i], w_far + still_far[side, 0, i]
                    m_own = power(w_own) * still[side, 1, i]
                    m_far = power(w_far) * still_far[side, 1, i]
                    flux[side, m, i] = jnp.where(
                        inside[side], (m_own + m_far) * (s_far - s_own), 0.0
                    )
            return carry

        for p in range(PARTS):
            for copy in halo_copies(step, p):
                copy.wait_recv()
        lax.fori_loop(0, BLOCKS, edge_flux, 0, unroll=2)

    def flows(step, m):
        top, bottom = sub == 0, sub == 7
        first, last = lane == 0, lane == 127

        def block(i, carry):
            carry = list(carry)
            base = pl.multiple_of(i * (128 * CHUNKS), 128 * CHUNKS)
            for j in range(CHUNKS):
                cols = pl.ds(base + j * 128, 128)
                w = [wat[m, h * 8:h * 8 + 8, cols] for h in range(2)]
                s = [bed[h * 8:h * 8 + 8, cols] + w[h] for h in range(2)]
                mo = [power(w[h]) * ivn[h * 8:h * 8 + 8, cols] for h in range(2)]
                s_dn = [pltpu.roll(v, 1, 0) for v in s]
                m_dn = [pltpu.roll(v, 1, 0) for v in mo]
                fv0 = jnp.where(top, 0.0, (m_dn[0] + mo[0]) * (s_dn[0] - s[0]))
                fv1 = (jnp.where(top, m_dn[0], m_dn[1]) + mo[1]) * (
                    jnp.where(top, s_dn[0], s_dn[1]) - s[1]
                )
                up0, up1 = pltpu.roll(fv0, 7, 0), pltpu.roll(fv1, 7, 0)
                nv = [
                    fv0 - jnp.where(bottom, up1, up0),
                    fv1 - jnp.where(bottom, 0.0, up1),
                ]
                for h in range(2):
                    s_prev, m_prev, f_prev, sum_prev = carry[h * 4:h * 4 + 4]
                    s_rt, m_rt = pltpu.roll(s[h], 1, 1), pltpu.roll(mo[h], 1, 1)
                    f = (jnp.where(first, m_prev, m_rt) + mo[h]) * (
                        jnp.where(first, s_prev, s_rt) - s[h]
                    )
                    f_lt = pltpu.roll(f, 127, 1)
                    wet[m, h * 8:h * 8 + 8, cols] = sum_prev - jnp.where(last, f_lt, f_prev)
                    total = (w[h] + rain[m, h * 8:h * 8 + 8, cols]) + (nv[h] + f)
                    carry[h * 4:h * 4 + 4] = [s_rt, m_rt, f_lt, total]
            return tuple(carry)

        zero = jnp.zeros((8, 128), F32)
        start = []
        for h in range(2):
            rows = slice(h * 8, h * 8 + 8)
            start += [bed[rows, 0:128] + wat[m, rows, 0:128], zero, zero, zero]
        carry = lax.fori_loop(0, COLS // 128 // CHUNKS, block, tuple(start))
        for h in range(2):
            f_prev, sum_prev = carry[h * 4 + 2:h * 4 + 4]
            wet[m, h * 8:h * 8 + 8, COLS:COLS + 128] = sum_prev - jnp.where(last, 0.0, f_prev)

    def drain(step):
        found = []
        for m in range(MEMB):
            now = [pool[m, v] * par[0, v] for v in range(2)]
            value = jnp.full((8, 128), FAR, F32)
            for j in range(LAKE_DEV // 4):
                row = spread(now[j // 8][j % 8:j % 8 + 1, :])
                value = jnp.where(code_row == j, lanes_of(row, code_lane), value)
            found.append(value)

        def set_levels(i, turned):
            for n in range(8):
                for m in range(MEMB):
                    level[m, i, n] = spread(turned[m][:, n:n + 1])
            return [pltpu.roll(value, 120, 1) for value in turned]

        def block(i, turned):
            turned = set_levels(i + 1, turned)
            base = pl.multiple_of(i * 1024, 1024)
            for g in range(4):
                for m in range(MEMB):
                    for h in range(2):
                        rows = slice(h * 8, h * 8 + 8)
                        low = level[m, i, 2 * g + h]
                        leaf = None
                        for j in (2 * g, 2 * g + 1):
                            cols = pl.ds(base + j * 128, 128)
                            w = wet[m, rows, pl.ds(base + j * 128 + 128, 128)]
                            over = spread(flux[h, m, i, j:j + 1, :])
                            w = w + jnp.where(sub == 7 * h, over, 0.0)
                            excess = jnp.maximum((bed[rows, cols] + w) - low, 0.0)
                            taken = (DRAIN * w) * (excess / (1.0 + excess))
                            left = w - taken
                            if step < STEPS - 1:
                                wat[m, rows, cols] = left
                                r = 0 if h == 0 else 7
                                edge[step + 1, h, m, i, j:j + 1, :] = left[r:r + 1, :]
                            else:
                                water[m, rows, cols] = left
                            leaf = taken if leaf is None else leaf + taken
                        part[m, i, 2 * g + h] = leaf
            return tuple(turned)

        turned = tuple(set_levels(0, found))
        for p in range(PARTS):
            turned = lax.fori_loop(p * SPAN, p * SPAN + SPAN, block, turned)
            if step < STEPS - 1:
                for copy in halo_copies(step + 1, p):
                    copy.start()
        sums = []
        for m in range(MEMB):
            groups = []
            for i in range(BLOCKS):
                leaves = [part[m, i, n] for n in range(8)]
                for bit in (1, 2, 4):
                    leaves = [
                        merge(leaves[n], leaves[n + 1], lane, bit, 1)
                        for n in range(0, len(leaves), 2)
                    ]
                groups.append(leaves[0])
            for bit in (8, 16, 32, 64):
                groups = [
                    merge(groups[n], groups[n + 1], lane, bit, 1) for n in range(0, len(groups), 2)
                ]
            sums.append(groups[0])
        return sums

    def tell(step, sums):
        picked = [jnp.zeros((8, 128), F32) for _ in range(MEMB)]
        for k in range(8):
            here = src_sub == k
            for m in range(MEMB):
                row = spread(sums[m][k:k + 1, :])
                picked[m] = jnp.where(here, lanes_of(row, src_lane), picked[m])
        for m in range(MEMB):
            msg[step, m] = picked[m][0:2, :]
        for peer in peers:
            pltpu.make_async_remote_copy(
                msg.at[step], got.at[step, me], ssem.at[step], rsem.at[step],
                device_id={"tiles": peer}, device_id_type=MESH,
            ).start()
        pltpu.make_async_copy(msg.at[step], got.at[step, me], rsem.at[step]).start()

    def hear(step):
        pltpu.make_async_copy(got.at[step], got.at[step], rsem.at[step]).wait()
        places = [pos[n] for n in range(TILES // 4)]
        for m in range(MEMB):
            values = [
                jnp.concatenate([got[step, 4 * n + d, m] for d in range(4)], axis=0)
                for n in range(TILES // 4)
            ]
            for j in range(LAKE_DEV // 4):
                leaves = []
                for p in range(4 * j, 4 * j + 4):
                    terms = [
                        jnp.where(places[n] == float(p), values[n], 0.0) for n in range(TILES // 4)
                    ]
                    leaves.append(total_of(terms))
                for bit in (32, 64):
                    leaves = [
                        merge(leaves[n], leaves[n + 1], lane, bit, 1)
                        for n in range(0, len(leaves), 2)
                    ]
                lines[m, j * 8:j * 8 + 8, :] = leaves[0]
        for m in range(MEMB):
            for v in range(2):
                lateral = total_of([lines[m, pl.ds(v * 64 + r, 8, stride=8), :] for r in range(8)])
                full = pool[m, v] + lateral * (1.0 / 256.0)
                out = par[1, v] * full
                above = total_of(
                    [chain[k, v] * pltpu.roll(out, k + 1, 1) for k in range(DEPTH - 1)]
                )
                out = out + par[1, v] * above
                pool[m, v] = full + above - out
                outf[m, v] = outf[m, v] + out

    for side in (0, 1):
        still_copies[side].start()
    for p in range(PARTS):
        for copy in halo_copies(0, p):
            copy.start()
    for m in range(MEMB):
        flows(0, m)

    pltpu.make_async_copy(greet, greet, isem).wait()
    for n in range(TILES // 4):
        pos[n] = jnp.concatenate([greet[4 * n + d, 0:2, :] for d in range(4)], axis=0)
    for k in range(4):
        pick = (lane & 15) * 4 + k
        for b in range(4):
            tile = jnp.zeros((8, 128), F32)
            for kind in range(5):
                rows = greet[b * 8:b * 8 + 8, 2 + kind, :]
                tile = jnp.where((lane >> 4) == kind, lanes_of(rows, pick), tile)
            turn[k * 32 + b * 8:k * 32 + b * 8 + 8, :] = tile
    turn[...] = jnp.transpose(turn[...])
    for v in range(2):
        used = sub + 8 * v < LAKE_DEV // 4
        rows = [turn[16 * kind + 8 * v:16 * kind + 8 * v + 8, :] for kind in range(5)]
        for m in range(MEMB):
            pool[m, v] = rows[m]
            outf[m, v] = jnp.zeros((8, 128), F32)
            lines[m, 64 + 8 * v:72 + 8 * v, :] = jnp.zeros((8, 128), F32)
            lines[m, 80 + 24 * v:104 + 24 * v, :] = jnp.zeros((24, 128), F32)
        par[0, v] = 1.0 / jnp.where(used, rows[2], 1.0)
        par[1, v] = rows[3]
        share = rows[3] * rows[4]
        run = rows[4]
        for k in range(DEPTH - 1):
            chain[k, v] = run
            run = run * pltpu.roll(share, k + 1, 1)

    for copy in still_copies:
        copy.wait_recv()
    for step in range(STEPS):
        edge_flows(step)
        if step > 0:
            hear(step - 1)
        sums = drain(step)
        tell(step, sums)
        if step < STEPS - 1:
            for m in range(MEMB):
                flows(step + 1, m)
    hear(STEPS - 1)

    pick = (lane & 3) * 32 + me
    own = [jnp.zeros((8, 128), F32) for _ in range(2)]
    for m in range(MEMB):
        for j in range(LAKE_DEV // 4):
            here = (lane >> 2) == j
            v, r = j // 8, j % 8
            own[0] = jnp.where(
                here & (sub == m), lanes_of(spread(pool[m, v, r:r + 1, :]), pick), own[0]
            )
            own[1] = own[1] + jnp.where(here, lanes_of(spread(outf[m, v, r:r + 1, :]), pick), 0.0)
    emsg[...] = own[1]
    for other in others:
        pltpu.make_async_remote_copy(
            emsg, egot.at[ye], esend, erecv, device_id={"ens": other}, device_id_type=MESH
        ).start()
    pltpu.make_async_copy(emsg, egot.at[ye], erecv).start()
    new_storage[...] = own[0][0:2, 0:LAKE_DEV]
    pltpu.make_async_copy(greet.at[1:], greet.at[1:], psem).wait()
    for copy in still_copies:
        copy.wait_send()
    for step in range(STEPS):
        for p in range(PARTS):
            for copy in halo_copies(step, p):
                copy.wait_send()
        pltpu.make_async_copy(got.at[step, 1:], got.at[step, 1:], ssem.at[step]).wait()
    pltpu.make_async_copy(egot, egot, erecv).wait()
    total = (egot[0] + egot[1] + egot[2] + egot[3]) * (1.0 / (MEMB * ENS))
    ens_outflow[...] = total[0:1, 0:LAKE_DEV]
    pltpu.make_async_copy(egot.at[1:], egot.at[1:], esend).wait()


def hand_out(water, pool, outflow, new_depth, new_storage, ens_outflow, sem):
    copies = [
        pltpu.make_async_copy(a, b, sem.at[n])
        for n, (a, b) in enumerate(
            [
                (water.at[0], new_depth.at[0]), (water.at[1], new_depth.at[1]),
                (pool, new_storage), (outflow, ens_outflow),
            ]
        )
    ]
    for copy in copies:
        copy.start()
    for copy in copies:
        copy.wait()


def shards(
    depth, bed, rain, rough_class, class_n, contact_seg, contact_lake, lake_slot,
    storage, area, release, upstream_link,
):
    far = pl.BlockSpec(memory_space=pltpu.HBM)
    vmem = pl.BlockSpec(memory_space=pltpu.VMEM)
    dma = pltpu.SemaphoreType.DMA
    results = pl.pallas_call(
        kernel,
        out_shape=(
            jax.ShapeDtypeStruct((MEMB, ROWS, COLS), F32),
            jax.ShapeDtypeStruct((MEMB, LAKE_DEV), F32),
            jax.ShapeDtypeStruct((1, LAKE_DEV), F32),
        ),
        in_specs=[far] * 12,
        out_specs=(vmem, vmem, vmem),
        scratch_shapes=[
            pltpu.VMEM((MEMB, ROWS, COLS), F32),
            pltpu.VMEM((MEMB, ROWS, COLS), F32),
            pltpu.VMEM((ROWS, COLS), F32),
            pltpu.VMEM((ROWS, COLS), F32),
            pltpu.VMEM((MEMB, ROWS, COLS + 128), F32),
            pltpu.VMEM((ROWS, COLS), I32),
            pltpu.SMEM((1, 8, TILES), I32),
            pltpu.SMEM((1, 8, TILES), I32),
            pltpu.SMEM((TILES * LAKE_DEV,), I32),
            pltpu.VMEM((1, 16), F32),
            pltpu.VMEM((MEMB, LAKE_DEV), F32),
            pltpu.VMEM((1, LAKE_DEV), F32),
            pltpu.VMEM((1, LAKE_DEV), F32),
            pltpu.VMEM((1, LAKE_DEV), I32),
            pltpu.VMEM((8, 128), F32),
            pltpu.VMEM((TILES, 8, 128), F32),
            pltpu.VMEM((128, 128), F32),
            pltpu.VMEM((TILES // 4, 8, 128), F32),
            pltpu.VMEM((MEMB, 2, 8, 128), F32),
            pltpu.VMEM((MEMB, 2, 8, 128), F32),
            pltpu.VMEM((2, 2, 8, 128), F32),
            pltpu.VMEM((DEPTH - 1, 2, 8, 128), F32),
            pltpu.VMEM((2, 2, BLOCKS, 8, 128), F32),
            pltpu.VMEM((2, 2, BLOCKS, 8, 128), F32),
            pltpu.VMEM((STEPS, 2, MEMB, BLOCKS, 8, 128), F32),
            pltpu.VMEM((STEPS, 2, MEMB, BLOCKS, 8, 128), F32),
            pltpu.VMEM((2, MEMB, BLOCKS, 8, 128), F32),
            pltpu.VMEM((MEMB, BLOCKS + 1, 8, 8, 128), F32),
            pltpu.VMEM((MEMB, BLOCKS, 8, 8, 128), F32),
            pltpu.VMEM((MEMB, 128, 128), F32),
            pltpu.VMEM((STEPS, MEMB, 2, 128), F32),
            pltpu.VMEM((STEPS, TILES, MEMB, 2, 128), F32),
            pltpu.VMEM((8, 128), F32),
            pltpu.VMEM((ENS, 8, 128), F32),
            dma((12,)),
            dma,
            dma,
            dma((STEPS,)),
            dma((STEPS,)),
            dma((STEPS, 2, PARTS)),
            dma((STEPS, 2, PARTS)),
            dma((2,)),
            dma((2,)),
            dma,
            dma,
        ],
        compiler_params=pltpu.CompilerParams(
            collective_id=0, has_side_effects=True, vmem_limit_bytes=40 * 1024 * 1024
        ),
    )(
        *[
            pltpu.with_memory_space_constraint(a, pltpu.HBM)
            for a in (
                depth, bed, rain, rough_class, class_n.reshape(1, -1),
                contact_seg.transpose(0, 2, 1), contact_lake.transpose(0, 2, 1),
                lake_slot, storage, area.reshape(1, -1), release.reshape(1, -1),
                upstream_link.reshape(1, -1),
            )
        ]
    )
    water, pool, outflow = pl.pallas_call(
        hand_out,
        out_shape=[jax.ShapeDtypeStruct(r.shape, r.dtype) for r in results],
        in_specs=[vmem] * 3,
        out_specs=(far, far, far),
        scratch_shapes=[dma((4,))],
        compiler_params=pltpu.CompilerParams(vmem_limit_bytes=1024 * 1024),
    )(*results)
    return water, pool, outflow.reshape(-1)


def solution(mesh):
    return jax.shard_map(
        shards,
        mesh=mesh,
        in_specs=(
            P("ens", "tiles", None),
            P("tiles", None),
            P("ens", "tiles", None),
            P("tiles", None),
            P(),
            P("tiles", None, None),
            P("tiles", None, None),
            P(),
            P("ens", "tiles"),
            P("tiles"),
            P("tiles"),
            P("tiles"),
        ),
        out_specs=(P("ens", "tiles", None), P("ens", "tiles"), P("tiles")),
        check_vma=False,
    )
```

```python
import jax
import jax.numpy as jnp
from jax import lax
from jax.experimental import pallas as pl
from jax.experimental.pallas import tpu as pltpu
from jax.sharding import PartitionSpec as P

STEPS = 4
TILES = 32
ENS = 4
MEMB = 2
ROWS = 16
COLS = 16384
BLOCKS = 16
PARTS = 2
CHUNKS = 16
DEPTH = 16
SPAN = BLOCKS // PARTS
LAKE_DEV = 40
FLOW = 0.035
DRAIN = 0.4
FAR = 3.0e38
MESH = pl.DeviceIdType.MESH
F32 = jnp.float32
I32 = jnp.int32


def iota(axis):
    return lax.broadcasted_iota(I32, (8, 128), axis)


def merge(a, b, index, bit, axis):
    odd = (index & bit) != 0
    return jnp.where(odd, b, a) + pltpu.roll(jnp.where(odd, a, b), bit, axis)


def total_of(terms):
    while len(terms) > 1:
        pairs = [terms[n] + terms[n + 1] for n in range(0, len(terms) - 1, 2)]
        terms = pairs + ([terms[-1]] if len(terms) % 2 else [])
    return terms[0]


def spread(row):
    return jnp.broadcast_to(row, (8, 128))


def lanes_of(table, index):
    return jnp.take_along_axis(table, index, axis=1)


def power(water):
    return water * jnp.exp2(jnp.log2(jnp.abs(water)) * (2.0 / 3.0))


def peer_offsets():
    near = {0: 0, 1: 1, 2: 2, 3: 1}
    found = [
        (z, x, c) for z in range(4) for x in range(4) for c in range(2) if (z, x, c) != (0, 0, 0)
    ]
    return sorted(found, key=lambda o: (-near[o[0]] - near[o[1]], o))


def kernel(
    depth, bed_in, rain_in, rough, class_n, contact_seg, contact_lake, lake_slot,
    storage, area, release, link,
    water, new_storage, ens_outflow,
    wat, rain, bed, ivn, wet, rgh,
    seg_s, lake_s, slot_s, cls_v, sto_v, are_v, rel_v, lnk_v,
    hello, greet, turn, pos, pool, outf, par, chain,
    still, still_far, edge, halo, flux, level, part, lines, msg, got, emsg, egot, share, shared,
    lsem, psem, isem, ssem, rsem, hsend, hrecv, bsend, brecv, esend, erecv, psend, precv, all_in,
):
    me = lax.axis_index("tiles")
    ye = lax.axis_index("ens")
    sub, lane = iota(0), iota(1)
    before, after = lax.rem(me + TILES - 1, TILES), lax.rem(me + 1, TILES)
    z, x, core = me // 8, (me // 2) % 4, me % 2
    peers = [
        (lax.rem(z + dz, 4) * 4 + lax.rem(x + dx, 4)) * 2 + lax.rem(core + dc, 2)
        for dz, dx, dc in peer_offsets()
    ]
    others = [lax.rem(ye + k, ENS) for k in range(1, ENS)]
    strangers = [{"tiles": peer, "ens": others[k]} for k in (1, 0, 2) for peer in peers + [me]]

    smalls = [
        (contact_seg, seg_s), (contact_lake, lake_s), (lake_slot, slot_s), (class_n, cls_v),
        (storage, sto_v), (area, are_v), (release, rel_v), (link, lnk_v),
    ]
    bigs = [(rough, rgh), (bed_in, bed), (depth, wat), (rain_in, rain)]
    loads = [pltpu.make_async_copy(a, b, lsem.at[i]) for i, (a, b) in enumerate(smalls + bigs)]
    for load in loads:
        load.start()

    barrier = pltpu.get_barrier_semaphore()
    for peer in peers:
        pl.semaphore_signal(barrier, inc=1, device_id={"tiles": peer}, device_id_type=MESH)
    for other in others:
        pl.semaphore_signal(barrier, inc=1, device_id={"ens": other}, device_id_type=MESH)

    for load in loads[: len(smalls)]:
        load.wait()

    seg_id = ((lane & 1) * 8 + sub) * 64 + (lane >> 1)
    contact_id = (lane & 31) * 8 + sub * 4 + (lane >> 5)

    def read_contacts(e, carry):
        code, from_seg, where_to = carry
        for c in range(8):
            seg = seg_s[0, c, e]
            lake = lake_s[0, c, e]
            live = lake >= 0
            place = slot_s[jnp.maximum(lake, 0)] - e * LAKE_DEV
            code = jnp.where(seg_id == seg, jnp.where(live, place * 32 + e, -1), code)
            mine = (contact_id == e * 8 + c) & (sub < 2)
            from_seg = jnp.where(mine, seg, from_seg)
            where_to = jnp.where(mine, jnp.where(live, place, -1), where_to)
        return code, from_seg, where_to

    none = jnp.full((8, 128), -1, I32)
    code, from_seg, where_to = lax.fori_loop(
        0, TILES, read_contacts, (none, jnp.zeros((8, 128), I32), none)
    )
    code_row, code_lane = code >> 7, code & 127
    src_sub = (from_seg >> 6) & 7
    src_lane = (from_seg & 63) * 2 + (from_seg >> 9)

    hello[...] = jnp.zeros((8, 128), F32)
    hello[0:2, :] = where_to.astype(F32)[0:2, :]
    hello[2:4, 0:LAKE_DEV] = sto_v[...]
    hello[4:5, 0:LAKE_DEV] = are_v[...]
    hello[5:6, 0:LAKE_DEV] = rel_v[...]
    hello[6:7, 0:LAKE_DEV] = lnk_v[...].astype(F32)

    for load in loads[len(smalls):]:
        load.wait()
    inverse = (0.5 * FLOW) / cls_v[...]
    classes = [spread(inverse[:, n:n + 1]) for n in range(16)]

    def inverse_of(index):
        found = classes
        for bit in (1, 2, 4, 8):
            odd = (index & bit) != 0
            found = [jnp.where(odd, found[n + 1], found[n]) for n in range(0, len(found), 2)]
        return found[0]

    def read_rough(i, carry):
        base = pl.multiple_of(i * 1024, 1024)
        for j in range(8):
            cols = pl.ds(base + j * 128, 128)
            for half in range(2):
                rows = slice(half * 8, half * 8 + 8)
                ivn[rows, cols] = inverse_of(rgh[rows, cols])
            for side, row in ((0, 0), (1, 15)):
                edge[0, side, 0, i, j:j + 1, :] = wat[0, row:row + 1, cols]
                edge[0, side, 1, i, j:j + 1, :] = wat[1, row:row + 1, cols]
                still[side, 0, i, j:j + 1, :] = bed[row:row + 1, cols]
                still[side, 1, i, j:j + 1, :] = ivn[row:row + 1, cols]
        return carry


    pl.semaphore_wait(barrier, TILES - 1 + ENS - 1)
    for other in others:
        pl.semaphore_signal(all_in, inc=1, device_id={"ens": other}, device_id_type=MESH)
    for peer in peers:
        pltpu.make_async_remote_copy(
            hello, greet.at[me], psem, isem, device_id={"tiles": peer}, device_id_type=MESH
        ).start()
    pltpu.make_async_copy(hello, greet.at[me], isem).start()
    lax.fori_loop(0, BLOCKS, read_rough, 0)

    def beside(side):
        return {"tiles": (before, after)[side]}

    still_copies = [
        pltpu.make_async_remote_copy(
            still.at[side], still_far.at[1 - side], bsend.at[side], brecv.at[side],
            device_id=beside(side), device_id_type=MESH,
        )
        for side in (0, 1)
    ]

    def halo_copies(step, p):
        at = pl.ds(p * SPAN, SPAN)
        return [
            pltpu.make_async_remote_copy(
                edge.at[step, side, :, at], halo.at[step, 1 - side, :, at],
                hsend.at[step, side, p], hrecv.at[step, side, p],
                device_id=beside(side), device_id_type=MESH,
            )
            for side in (0, 1)
        ]

    def edge_flows(step):
        inside = (me > 0, me < TILES - 1)

        def edge_flux(i, carry):
            for side in (0, 1):
                for m in range(MEMB):
                    w_own, w_far = edge[step, side, m, i], halo[step, side, m, i]
                    s_own, s_far = w_own + still[side, 0, i], w_far + still_far[side, 0, i]
                    m_own = power(w_own) * still[side, 1, i]
                    m_far = power(w_far) * still_far[side, 1, i]
                    flux[side, m, i] = jnp.where(
                        inside[side], (m_own + m_far) * (s_far - s_own), 0.0
                    )
            return carry

        for p in range(PARTS):
            for copy in halo_copies(step, p):
                copy.wait_recv()
        lax.fori_loop(0, BLOCKS, edge_flux, 0, unroll=2)

    def flows(step, m):
        top, bottom = sub == 0, sub == 7
        first, last = lane == 0, lane == 127

        def block(i, carry):
            carry = list(carry)
            base = pl.multiple_of(i * (128 * CHUNKS), 128 * CHUNKS)
            for j in range(CHUNKS):
                cols = pl.ds(base + j * 128, 128)
                w = [wat[m, h * 8:h * 8 + 8, cols] for h in range(2)]
                s = [bed[h * 8:h * 8 + 8, cols] + w[h] for h in range(2)]
                mo = [power(w[h]) * ivn[h * 8:h * 8 + 8, cols] for h in range(2)]
                s_dn = [pltpu.roll(v, 1, 0) for v in s]
                m_dn = [pltpu.roll(v, 1, 0) for v in mo]
                fv0 = jnp.where(top, 0.0, (m_dn[0] + mo[0]) * (s_dn[0] - s[0]))
                fv1 = (jnp.where(top, m_dn[0], m_dn[1]) + mo[1]) * (
                    jnp.where(top, s_dn[0], s_dn[1]) - s[1]
                )
                up0, up1 = pltpu.roll(fv0, 7, 0), pltpu.roll(fv1, 7, 0)
                nv = [
                    fv0 - jnp.where(bottom, up1, up0),
                    fv1 - jnp.where(bottom, 0.0, up1),
                ]
                for h in range(2):
                    s_prev, m_prev, f_prev, sum_prev = carry[h * 4:h * 4 + 4]
                    s_rt, m_rt = pltpu.roll(s[h], 1, 1), pltpu.roll(mo[h], 1, 1)
                    f = (jnp.where(first, m_prev, m_rt) + mo[h]) * (
                        jnp.where(first, s_prev, s_rt) - s[h]
                    )
                    f_lt = pltpu.roll(f, 127, 1)
                    wet[m, h * 8:h * 8 + 8, cols] = sum_prev - jnp.where(last, f_lt, f_prev)
                    total = (w[h] + rain[m, h * 8:h * 8 + 8, cols]) + (nv[h] + f)
                    carry[h * 4:h * 4 + 4] = [s_rt, m_rt, f_lt, total]
            return tuple(carry)

        zero = jnp.zeros((8, 128), F32)
        start = []
        for h in range(2):
            rows = slice(h * 8, h * 8 + 8)
            start += [bed[rows, 0:128] + wat[m, rows, 0:128], zero, zero, zero]
        carry = lax.fori_loop(0, COLS // 128 // CHUNKS, block, tuple(start))
        for h in range(2):
            f_prev, sum_prev = carry[h * 4 + 2:h * 4 + 4]
            wet[m, h * 8:h * 8 + 8, COLS:COLS + 128] = sum_prev - jnp.where(last, 0.0, f_prev)

    def drain(step):
        found = []
        for m in range(MEMB):
            now = [pool[m, v] * par[0, v] for v in range(2)]
            value = jnp.full((8, 128), FAR, F32)
            for j in range(LAKE_DEV // 4):
                row = spread(now[j // 8][j % 8:j % 8 + 1, :])
                value = jnp.where(code_row == j, lanes_of(row, code_lane), value)
            found.append(value)

        def set_levels(i, turned):
            for n in range(8):
                for m in range(MEMB):
                    level[m, i, n] = spread(turned[m][:, n:n + 1])
            return [pltpu.roll(value, 120, 1) for value in turned]

        def block(i, turned):
            turned = set_levels(i + 1, turned)
            base = pl.multiple_of(i * 1024, 1024)
            for g in range(4):
                for m in range(MEMB):
                    for h in range(2):
                        rows = slice(h * 8, h * 8 + 8)
                        low = level[m, i, 2 * g + h]
                        leaf = None
                        for j in (2 * g, 2 * g + 1):
                            cols = pl.ds(base + j * 128, 128)
                            w = wet[m, rows, pl.ds(base + j * 128 + 128, 128)]
                            over = spread(flux[h, m, i, j:j + 1, :])
                            w = w + jnp.where(sub == 7 * h, over, 0.0)
                            excess = jnp.maximum((bed[rows, cols] + w) - low, 0.0)
                            taken = (DRAIN * w) * (excess / (1.0 + excess))
                            left = w - taken
                            if step < STEPS - 1:
                                wat[m, rows, cols] = left
                                r = 0 if h == 0 else 7
                                edge[step + 1, h, m, i, j:j + 1, :] = left[r:r + 1, :]
                            else:
                                water[m, rows, cols] = left
                            leaf = taken if leaf is None else leaf + taken
                        part[m, i, 2 * g + h] = leaf
            return tuple(turned)

        turned = tuple(set_levels(0, found))
        for p in range(PARTS):
            turned = lax.fori_loop(p * SPAN, p * SPAN + SPAN, block, turned, unroll=2)
            if step < STEPS - 1:
                for copy in halo_copies(step + 1, p):
                    copy.start()
        sums = []
        for m in range(MEMB):
            groups = []
            for i in range(BLOCKS):
                leaves = [part[m, i, n] for n in range(8)]
                for bit in (1, 2, 4):
                    leaves = [
                        merge(leaves[n], leaves[n + 1], lane, bit, 1)
                        for n in range(0, len(leaves), 2)
                    ]
                groups.append(leaves[0])
            for bit in (8, 16, 32, 64):
                groups = [
                    merge(groups[n], groups[n + 1], lane, bit, 1) for n in range(0, len(groups), 2)
                ]
            sums.append(groups[0])
        return sums

    def tell(step, sums):
        picked = [jnp.zeros((8, 128), F32) for _ in range(MEMB)]
        for k in range(8):
            here = src_sub == k
            for m in range(MEMB):
                row = spread(sums[m][k:k + 1, :])
                picked[m] = jnp.where(here, lanes_of(row, src_lane), picked[m])
        for m in range(MEMB):
            msg[step, m] = picked[m][0:2, :]
        for peer in peers:
            pltpu.make_async_remote_copy(
                msg.at[step], got.at[step, me], ssem.at[step], rsem.at[step],
                device_id={"tiles": peer}, device_id_type=MESH,
            ).start()
        pltpu.make_async_copy(msg.at[step], got.at[step, me], rsem.at[step]).start()
        if step == STEPS - 1:
            emsg[...] = (picked[0] + picked[1])[0:2, :]
            pl.semaphore_wait(all_in, ENS - 1)
            for stranger in strangers:
                pltpu.make_async_remote_copy(
                    emsg, egot.at[ye, me], esend, erecv, device_id=stranger, device_id_type=MESH
                ).start()

    places = []

    def slot_sums(values, m):
        for j in range(LAKE_DEV // 4):
            leaves = [
                total_of([jnp.where(at == float(p), v, 0.0) for at, v in zip(places, values)])
                for p in range(4 * j, 4 * j + 4)
            ]
            for bit in (32, 64):
                leaves = [
                    merge(leaves[n], leaves[n + 1], lane, bit, 1) for n in range(0, len(leaves), 2)
                ]
            lines[m, j * 8:j * 8 + 8, :] = leaves[0]

    def cascade(held, m, v):
        lateral = total_of([lines[m, pl.ds(v * 64 + r, 8, stride=8), :] for r in range(8)])
        full = held + lateral * (1.0 / 256.0)
        out = par[1, v] * full
        above = total_of([chain[k, v] * pltpu.roll(out, k + 1, 1) for k in range(DEPTH - 1)])
        out = out + par[1, v] * above
        return full + above - out, out

    def heard(step):
        pltpu.make_async_copy(got.at[step], got.at[step], rsem.at[step]).wait()
        places[:] = [pos[n] for n in range(TILES // 4)]
        return [
            [
                jnp.concatenate([got[step, 4 * n + d, m] for d in range(4)], axis=0)
                for n in range(TILES // 4)
            ]
            for m in range(MEMB)
        ]

    def hear(step):
        values = heard(step)
        for m in range(MEMB):
            slot_sums(values[m], m)
        for m in range(MEMB):
            for v in range(2):
                pool[m, v], out = cascade(pool[m, v], m, v)
                if step < STEPS - 1:
                    outf[m, v] = outf[m, v] + out
        return values

    def share_copies():
        return [
            pltpu.make_async_remote_copy(
                share, shared.at[ye], psend, precv, device_id={"ens": other}, device_id_type=MESH
            )
            for other in others
        ]

    def share_start():
        for v in range(2):
            share[0, v] = pool[0, v] + pool[1, v]
            share[1, v] = outf[0, v] + outf[1, v]
        for copy in share_copies():
            copy.start()
        pltpu.make_async_copy(share, shared.at[ye], precv).start()

    for side in (0, 1):
        still_copies[side].start()
    for p in range(PARTS):
        for copy in halo_copies(0, p):
            copy.start()
    for m in range(MEMB):
        flows(0, m)

    pltpu.make_async_copy(greet, greet, isem).wait()
    for n in range(TILES // 4):
        pos[n] = jnp.concatenate([greet[4 * n + d, 0:2, :] for d in range(4)], axis=0)
    for k in range(4):
        pick = (lane & 15) * 4 + k
        for b in range(4):
            tile = jnp.zeros((8, 128), F32)
            for kind in range(5):
                rows = greet[b * 8:b * 8 + 8, 2 + kind, :]
                tile = jnp.where((lane >> 4) == kind, lanes_of(rows, pick), tile)
            turn[k * 32 + b * 8:k * 32 + b * 8 + 8, :] = tile
    turn[...] = jnp.transpose(turn[...])
    for m in range(MEMB + 1):
        lines[m, 80:128, :] = jnp.zeros((48, 128), F32)
    for v in range(2):
        used = sub + 8 * v < LAKE_DEV // 4
        rows = [turn[16 * kind + 8 * v:16 * kind + 8 * v + 8, :] for kind in range(5)]
        for m in range(MEMB):
            pool[m, v] = rows[m]
            outf[m, v] = jnp.zeros((8, 128), F32)
        par[0, v] = 1.0 / jnp.where(used, rows[2], 1.0)
        par[1, v] = rows[3]
        factor = rows[3] * rows[4]
        run = rows[4]
        for k in range(DEPTH - 1):
            chain[k, v] = run
            run = run * pltpu.roll(factor, k + 1, 1)

    for copy in still_copies:
        copy.wait_recv()
    for step in range(STEPS):
        edge_flows(step)
        if step > 0:
            hear(step - 1)
        sums = drain(step)
        tell(step, sums)
        if step == STEPS - 1:
            share_start()
        else:
            for m in range(MEMB):
                flows(step + 1, m)
    values = hear(STEPS - 1)

    pltpu.make_async_copy(shared, shared, precv).wait()
    pltpu.make_async_copy(egot.at[1:], egot.at[1:], erecv).wait()
    everyone = []
    for n in range(TILES // 4):
        mine = values[0][n] + values[1][n]
        everyone.append(
            total_of(
                [
                    jnp.where(
                        ye == y,
                        mine,
                        jnp.concatenate([egot[y, 4 * n + d] for d in range(4)], axis=0),
                    )
                    for y in range(ENS)
                ]
            )
        )
    slot_sums(everyone, MEMB)
    sum_of = [
        [total_of([shared[y, kind, v] for y in range(ENS)]) for v in range(2)] for kind in range(2)
    ]
    outflow = [sum_of[1][v] + cascade(sum_of[0][v], MEMB, v)[1] for v in range(2)]

    pick = (lane & 3) * 32 + me
    own = [jnp.zeros((8, 128), F32) for _ in range(2)]
    for j in range(LAKE_DEV // 4):
        here = (lane >> 2) == j
        v, r = j // 8, j % 8
        for m in range(MEMB):
            own[0] = jnp.where(
                here & (sub == m), lanes_of(spread(pool[m, v, r:r + 1, :]), pick), own[0]
            )
        own[1] = jnp.where(here, lanes_of(spread(outflow[v][r:r + 1, :]), pick), own[1])
    new_storage[...] = own[0][0:2, 0:LAKE_DEV]
    ens_outflow[...] = (own[1] * (1.0 / (MEMB * ENS)))[0:1, 0:LAKE_DEV]

    pltpu.make_async_copy(greet.at[1:], greet.at[1:], psem).wait()
    for copy in still_copies:
        copy.wait_send()
    for step in range(STEPS):
        for p in range(PARTS):
            for copy in halo_copies(step, p):
                copy.wait_send()
        pltpu.make_async_copy(got.at[step, 1:], got.at[step, 1:], ssem.at[step]).wait()
    pltpu.make_async_copy(shared.at[1:], shared.at[1:], psend).wait()
    pltpu.make_async_copy(egot.at[1:], egot.at[1:], esend).wait()


def hand_out(water, pool, outflow, new_depth, new_storage, ens_outflow, sem):
    copies = [
        pltpu.make_async_copy(a, b, sem.at[n])
        for n, (a, b) in enumerate(
            [
                (water.at[0], new_depth.at[0]), (water.at[1], new_depth.at[1]),
                (pool, new_storage), (outflow, ens_outflow),
            ]
        )
    ]
    for copy in copies:
        copy.start()
    for copy in copies:
        copy.wait()


def shards(
    depth, bed, rain, rough_class, class_n, contact_seg, contact_lake, lake_slot,
    storage, area, release, upstream_link,
):
    far = pl.BlockSpec(memory_space=pltpu.HBM)
    vmem = pl.BlockSpec(memory_space=pltpu.VMEM)
    dma = pltpu.SemaphoreType.DMA
    results = pl.pallas_call(
        kernel,
        out_shape=(
            jax.ShapeDtypeStruct((MEMB, ROWS, COLS), F32),
            jax.ShapeDtypeStruct((MEMB, LAKE_DEV), F32),
            jax.ShapeDtypeStruct((1, LAKE_DEV), F32),
        ),
        in_specs=[far] * 12,
        out_specs=(vmem, vmem, vmem),
        scratch_shapes=[
            pltpu.VMEM((MEMB, ROWS, COLS), F32),
            pltpu.VMEM((MEMB, ROWS, COLS), F32),
            pltpu.VMEM((ROWS, COLS), F32),
            pltpu.VMEM((ROWS, COLS), F32),
            pltpu.VMEM((MEMB, ROWS, COLS + 128), F32),
            pltpu.VMEM((ROWS, COLS), I32),
            pltpu.SMEM((1, 8, TILES), I32),
            pltpu.SMEM((1, 8, TILES), I32),
            pltpu.SMEM((TILES * LAKE_DEV,), I32),
            pltpu.VMEM((1, 16), F32),
            pltpu.VMEM((MEMB, LAKE_DEV), F32),
            pltpu.VMEM((1, LAKE_DEV), F32),
            pltpu.VMEM((1, LAKE_DEV), F32),
            pltpu.VMEM((1, LAKE_DEV), I32),
            pltpu.VMEM((8, 128), F32),
            pltpu.VMEM((TILES, 8, 128), F32),
            pltpu.VMEM((128, 128), F32),
            pltpu.VMEM((TILES // 4, 8, 128), F32),
            pltpu.VMEM((MEMB, 2, 8, 128), F32),
            pltpu.VMEM((MEMB, 2, 8, 128), F32),
            pltpu.VMEM((2, 2, 8, 128), F32),
            pltpu.VMEM((DEPTH - 1, 2, 8, 128), F32),
            pltpu.VMEM((2, 2, BLOCKS, 8, 128), F32),
            pltpu.VMEM((2, 2, BLOCKS, 8, 128), F32),
            pltpu.VMEM((STEPS, 2, MEMB, BLOCKS, 8, 128), F32),
            pltpu.VMEM((STEPS, 2, MEMB, BLOCKS, 8, 128), F32),
            pltpu.VMEM((2, MEMB, BLOCKS, 8, 128), F32),
            pltpu.VMEM((MEMB, BLOCKS + 1, 8, 8, 128), F32),
            pltpu.VMEM((MEMB, BLOCKS, 8, 8, 128), F32),
            pltpu.VMEM((MEMB + 1, 128, 128), F32),
            pltpu.VMEM((STEPS, MEMB, 2, 128), F32),
            pltpu.VMEM((STEPS, TILES, MEMB, 2, 128), F32),
            pltpu.VMEM((2, 128), F32),
            pltpu.VMEM((ENS, TILES, 2, 128), F32),
            pltpu.VMEM((2, 2, 8, 128), F32),
            pltpu.VMEM((ENS, 2, 2, 8, 128), F32),
            dma((12,)),
            dma,
            dma,
            dma((STEPS,)),
            dma((STEPS,)),
            dma((STEPS, 2, PARTS)),
            dma((STEPS, 2, PARTS)),
            dma((2,)),
            dma((2,)),
            dma,
            dma,
            dma,
            dma,
            pltpu.SemaphoreType.REGULAR,
        ],
        compiler_params=pltpu.CompilerParams(
            collective_id=0, has_side_effects=True, vmem_limit_bytes=40 * 1024 * 1024
        ),
    )(
        *[
            pltpu.with_memory_space_constraint(a, pltpu.HBM)
            for a in (
                depth, bed, rain, rough_class, class_n.reshape(1, -1),
                contact_seg.transpose(0, 2, 1), contact_lake.transpose(0, 2, 1),
                lake_slot, storage, area.reshape(1, -1), release.reshape(1, -1),
                upstream_link.reshape(1, -1),
            )
        ]
    )
    water, pool, outflow = pl.pallas_call(
        hand_out,
        out_shape=[jax.ShapeDtypeStruct(r.shape, r.dtype) for r in results],
        in_specs=[vmem] * 3,
        out_specs=(far, far, far),
        scratch_shapes=[dma((4,))],
        compiler_params=pltpu.CompilerParams(vmem_limit_bytes=1024 * 1024),
    )(*results)
    return water, pool, outflow.reshape(-1)


def solution(mesh):
    return jax.shard_map(
        shards,
        mesh=mesh,
        in_specs=(
            P("ens", "tiles", None),
            P("tiles", None),
            P("ens", "tiles", None),
            P("tiles", None),
            P(),
            P("tiles", None, None),
            P("tiles", None, None),
            P(),
            P("ens", "tiles"),
            P("tiles"),
            P("tiles"),
            P("tiles"),
        ),
        out_specs=(P("ens", "tiles", None), P("ens", "tiles"), P("tiles")),
        check_vma=False,
    )
```

```python
import jax
import jax.numpy as jnp
from jax import lax
from jax.experimental import pallas as pl
from jax.experimental.pallas import tpu as pltpu
from jax.sharding import PartitionSpec as P

STEPS = 4
TILES = 32
ENS = 4
MEMB = 2
ROWS = 16
COLS = 16384
BLOCKS = 16
PARTS = 2
CHUNKS = 16
DEPTH = 16
SPAN = BLOCKS // PARTS
LAKE_DEV = 40
FLOW = 0.035
DRAIN = 0.4
FAR = 3.0e38
MESH = pl.DeviceIdType.MESH
F32 = jnp.float32
I32 = jnp.int32


def iota(axis):
    return lax.broadcasted_iota(I32, (8, 128), axis)


def merge(a, b, index, bit, axis):
    odd = (index & bit) != 0
    return jnp.where(odd, b, a) + pltpu.roll(jnp.where(odd, a, b), bit, axis)


def total_of(terms):
    while len(terms) > 1:
        pairs = [terms[n] + terms[n + 1] for n in range(0, len(terms) - 1, 2)]
        terms = pairs + ([terms[-1]] if len(terms) % 2 else [])
    return terms[0]


def spread(row):
    return jnp.broadcast_to(row, (8, 128))


def lanes_of(table, index):
    return jnp.take_along_axis(table, index, axis=1)


def power(water):
    return water * jnp.exp2(jnp.log2(jnp.abs(water)) * (2.0 / 3.0))


def merge4(leaves, index, bit):
    low, high = (index & bit) != 0, (index & (2 * bit)) != 0
    terms = []
    for t in range(4):
        a, b, c, d = [leaves[(q + t) % 4] for q in range(4)]
        value = jnp.where(high, jnp.where(low, d, c), jnp.where(low, b, a))
        terms.append(pltpu.roll(value, t * bit, 1) if t else value)
    return total_of(terms)


def peer_offsets():
    near = {0: 0, 1: 1, 2: 2, 3: 1}
    found = [
        (z, x, c) for z in range(4) for x in range(4) for c in range(2) if (z, x, c) != (0, 0, 0)
    ]
    return sorted(found, key=lambda o: (-near[o[0]] - near[o[1]], o))


def kernel(
    depth, bed_in, rain_in, rough, class_n, contact_seg, contact_lake, lake_slot,
    storage, area, release, link,
    water, new_storage, ens_outflow,
    wat, rain, bed, ivn, wet, rgh,
    seg_s, lake_s, slot_s, cls_v, sto_v, are_v, rel_v, lnk_v,
    hello, greet, turn, pos, pool, outf, par, chain,
    still, still_far, edge, halo, flux, level, part, lines, msg, got, emsg, egot, share, shared,
    lsem, psem, isem, ssem, rsem, hsend, hrecv, bsend, brecv, esend, erecv, psend, precv, all_in,
):
    me = lax.axis_index("tiles")
    ye = lax.axis_index("ens")
    sub, lane = iota(0), iota(1)
    before, after = lax.rem(me + TILES - 1, TILES), lax.rem(me + 1, TILES)
    z, x, core = me // 8, (me // 2) % 4, me % 2
    peers = [
        (lax.rem(z + dz, 4) * 4 + lax.rem(x + dx, 4)) * 2 + lax.rem(core + dc, 2)
        for dz, dx, dc in peer_offsets()
    ]
    others = [lax.rem(ye + k, ENS) for k in range(1, ENS)]
    strangers = [{"tiles": peer, "ens": others[k]} for k in (1, 0, 2) for peer in peers + [me]]

    smalls = [
        (contact_seg, seg_s), (contact_lake, lake_s), (lake_slot, slot_s), (class_n, cls_v),
        (storage, sto_v), (area, are_v), (release, rel_v), (link, lnk_v),
    ]
    bigs = [(rough, rgh), (bed_in, bed), (depth, wat), (rain_in, rain)]
    loads = [pltpu.make_async_copy(a, b, lsem.at[i]) for i, (a, b) in enumerate(smalls + bigs)]
    for load in loads:
        load.start()

    barrier = pltpu.get_barrier_semaphore()
    for peer in peers:
        pl.semaphore_signal(barrier, inc=1, device_id={"tiles": peer}, device_id_type=MESH)
    for other in others:
        pl.semaphore_signal(barrier, inc=1, device_id={"ens": other}, device_id_type=MESH)

    for load in loads[: len(smalls)]:
        load.wait()

    seg_id = ((lane & 1) * 8 + sub) * 64 + (lane >> 1)
    contact_id = (lane & 31) * 8 + sub * 4 + (lane >> 5)

    def read_contacts(e, carry):
        code, from_seg, where_to = carry
        for c in range(8):
            seg = seg_s[0, c, e]
            lake = lake_s[0, c, e]
            live = lake >= 0
            place = slot_s[jnp.maximum(lake, 0)] - e * LAKE_DEV
            code = jnp.where(seg_id == seg, jnp.where(live, place * 32 + e, -1), code)
            mine = (contact_id == e * 8 + c) & (sub < 2)
            from_seg = jnp.where(mine, seg, from_seg)
            where_to = jnp.where(mine, jnp.where(live, place, -1), where_to)
        return code, from_seg, where_to

    none = jnp.full((8, 128), -1, I32)
    code, from_seg, where_to = lax.fori_loop(
        0, TILES, read_contacts, (none, jnp.zeros((8, 128), I32), none)
    )
    code_row, code_lane = code >> 7, code & 127
    src_sub = (from_seg >> 6) & 7
    src_lane = (from_seg & 63) * 2 + (from_seg >> 9)

    hello[...] = jnp.zeros((8, 128), F32)
    hello[0:2, :] = where_to.astype(F32)[0:2, :]
    hello[2:4, 0:LAKE_DEV] = sto_v[...]
    hello[4:5, 0:LAKE_DEV] = are_v[...]
    hello[5:6, 0:LAKE_DEV] = rel_v[...]
    hello[6:7, 0:LAKE_DEV] = lnk_v[...].astype(F32)

    for load in loads[len(smalls):]:
        load.wait()
    inverse = (0.5 * FLOW) / cls_v[...]
    classes = [spread(inverse[:, n:n + 1]) for n in range(16)]

    def inverse_of(index):
        found = classes
        for bit in (1, 2, 4, 8):
            odd = (index & bit) != 0
            found = [jnp.where(odd, found[n + 1], found[n]) for n in range(0, len(found), 2)]
        return found[0]

    def read_rough(i, carry):
        base = pl.multiple_of(i * 1024, 1024)
        for j in range(8):
            cols = pl.ds(base + j * 128, 128)
            for half in range(2):
                rows = slice(half * 8, half * 8 + 8)
                ivn[rows, cols] = inverse_of(rgh[rows, cols])
            for side, row in ((0, 0), (1, 15)):
                edge[0, side, 0, i, j:j + 1, :] = wat[0, row:row + 1, cols]
                edge[0, side, 1, i, j:j + 1, :] = wat[1, row:row + 1, cols]
                still[side, 0, i, j:j + 1, :] = bed[row:row + 1, cols]
                still[side, 1, i, j:j + 1, :] = ivn[row:row + 1, cols]
        return carry


    pl.semaphore_wait(barrier, TILES - 1 + ENS - 1)
    for other in others:
        pl.semaphore_signal(all_in, inc=1, device_id={"ens": other}, device_id_type=MESH)
    for peer in peers:
        pltpu.make_async_remote_copy(
            hello, greet.at[me], psem, isem, device_id={"tiles": peer}, device_id_type=MESH
        ).start()
    pltpu.make_async_copy(hello, greet.at[me], isem).start()
    lax.fori_loop(0, BLOCKS, read_rough, 0)

    def beside(side):
        return {"tiles": (before, after)[side]}

    still_copies = [
        pltpu.make_async_remote_copy(
            still.at[side], still_far.at[1 - side], bsend.at[side], brecv.at[side],
            device_id=beside(side), device_id_type=MESH,
        )
        for side in (0, 1)
    ]

    def halo_copies(step, p):
        at = pl.ds(p * SPAN, SPAN)
        return [
            pltpu.make_async_remote_copy(
                edge.at[step, side, :, at], halo.at[step, 1 - side, :, at],
                hsend.at[step, side, p], hrecv.at[step, side, p],
                device_id=beside(side), device_id_type=MESH,
            )
            for side in (0, 1)
        ]

    def edge_flows(step):
        inside = (me > 0, me < TILES - 1)

        def edge_flux(i, carry):
            for side in (0, 1):
                for m in range(MEMB):
                    w_own, w_far = edge[step, side, m, i], halo[step, side, m, i]
                    s_own, s_far = w_own + still[side, 0, i], w_far + still_far[side, 0, i]
                    m_own = power(w_own) * still[side, 1, i]
                    m_far = power(w_far) * still_far[side, 1, i]
                    flux[side, m, i] = jnp.where(
                        inside[side], (m_own + m_far) * (s_far - s_own), 0.0
                    )
            return carry

        for p in range(PARTS):
            for copy in halo_copies(step, p):
                copy.wait_recv()
        lax.fori_loop(0, BLOCKS, edge_flux, 0, unroll=2)

    def flows(step, m):
        top, bottom = sub == 0, sub == 7
        first, last = lane == 0, lane == 127

        def block(i, carry):
            carry = list(carry)
            base = pl.multiple_of(i * (128 * CHUNKS), 128 * CHUNKS)
            for j in range(CHUNKS):
                cols = pl.ds(base + j * 128, 128)
                w = [wat[m, h * 8:h * 8 + 8, cols] for h in range(2)]
                s = [bed[h * 8:h * 8 + 8, cols] + w[h] for h in range(2)]
                mo = [power(w[h]) * ivn[h * 8:h * 8 + 8, cols] for h in range(2)]
                s_dn = [pltpu.roll(v, 1, 0) for v in s]
                m_dn = [pltpu.roll(v, 1, 0) for v in mo]
                fv0 = jnp.where(top, 0.0, (m_dn[0] + mo[0]) * (s_dn[0] - s[0]))
                fv1 = (jnp.where(top, m_dn[0], m_dn[1]) + mo[1]) * (
                    jnp.where(top, s_dn[0], s_dn[1]) - s[1]
                )
                up0, up1 = pltpu.roll(fv0, 7, 0), pltpu.roll(fv1, 7, 0)
                nv = [
                    fv0 - jnp.where(bottom, up1, up0),
                    fv1 - jnp.where(bottom, 0.0, up1),
                ]
                for h in range(2):
                    s_prev, m_prev, f_prev, sum_prev = carry[h * 4:h * 4 + 4]
                    s_rt, m_rt = pltpu.roll(s[h], 1, 1), pltpu.roll(mo[h], 1, 1)
                    f = (jnp.where(first, m_prev, m_rt) + mo[h]) * (
                        jnp.where(first, s_prev, s_rt) - s[h]
                    )
                    f_lt = pltpu.roll(f, 127, 1)
                    wet[m, h * 8:h * 8 + 8, cols] = sum_prev - jnp.where(last, f_lt, f_prev)
                    total = (w[h] + rain[m, h * 8:h * 8 + 8, cols]) + (nv[h] + f)
                    carry[h * 4:h * 4 + 4] = [s_rt, m_rt, f_lt, total]
            return tuple(carry)

        zero = jnp.zeros((8, 128), F32)
        start = []
        for h in range(2):
            rows = slice(h * 8, h * 8 + 8)
            start += [bed[rows, 0:128] + wat[m, rows, 0:128], zero, zero, zero]
        carry = lax.fori_loop(0, COLS // 128 // CHUNKS, block, tuple(start))
        for h in range(2):
            f_prev, sum_prev = carry[h * 4 + 2:h * 4 + 4]
            wet[m, h * 8:h * 8 + 8, COLS:COLS + 128] = sum_prev - jnp.where(last, 0.0, f_prev)

    def drain(step):
        found = []
        for m in range(MEMB):
            now = [pool[m, v] * par[0, v] for v in range(2)]
            value = jnp.full((8, 128), FAR, F32)
            for j in range(LAKE_DEV // 4):
                row = spread(now[j // 8][j % 8:j % 8 + 1, :])
                value = jnp.where(code_row == j, lanes_of(row, code_lane), value)
            found.append(value)

        def set_levels(i, turned):
            for n in range(8):
                for m in range(MEMB):
                    level[m, i, n] = spread(turned[m][:, n:n + 1])
            return [pltpu.roll(value, 120, 1) for value in turned]

        def block(i, turned):
            turned = set_levels(i + 1, turned)
            base = pl.multiple_of(i * 1024, 1024)
            for g in range(4):
                for m in range(MEMB):
                    for h in range(2):
                        rows = slice(h * 8, h * 8 + 8)
                        low = level[m, i, 2 * g + h]
                        leaf = None
                        for j in (2 * g, 2 * g + 1):
                            cols = pl.ds(base + j * 128, 128)
                            w = wet[m, rows, pl.ds(base + j * 128 + 128, 128)]
                            over = spread(flux[h, m, i, j:j + 1, :])
                            w = w + jnp.where(sub == 7 * h, over, 0.0)
                            excess = jnp.maximum((bed[rows, cols] + w) - low, 0.0)
                            taken = (DRAIN * w) * (excess / (1.0 + excess))
                            left = w - taken
                            if step < STEPS - 1:
                                wat[m, rows, cols] = left
                                r = 0 if h == 0 else 7
                                edge[step + 1, h, m, i, j:j + 1, :] = left[r:r + 1, :]
                            else:
                                water[m, rows, cols] = left
                            leaf = taken if leaf is None else leaf + taken
                        part[m, i, 2 * g + h] = leaf
            return tuple(turned)

        turned = tuple(set_levels(0, found))
        for p in range(PARTS):
            turned = lax.fori_loop(p * SPAN, p * SPAN + SPAN, block, turned, unroll=4)
            if step < STEPS - 1:
                for copy in halo_copies(step + 1, p):
                    copy.start()
        sums = []
        for m in range(MEMB):
            groups = []
            for i in range(BLOCKS):
                leaves = [part[m, i, n] for n in range(8)]
                for bit in (1, 2, 4):
                    leaves = [
                        merge(leaves[n], leaves[n + 1], lane, bit, 1)
                        for n in range(0, len(leaves), 2)
                    ]
                groups.append(leaves[0])
            for bit in (8, 32):
                groups = [merge4(groups[n:n + 4], lane, bit) for n in range(0, len(groups), 4)]
            sums.append(groups[0])
        return sums

    def tell(step, sums):
        picked = [jnp.zeros((8, 128), F32) for _ in range(MEMB)]
        for k in range(8):
            here = src_sub == k
            for m in range(MEMB):
                row = spread(sums[m][k:k + 1, :])
                picked[m] = jnp.where(here, lanes_of(row, src_lane), picked[m])
        for m in range(MEMB):
            msg[step, m] = picked[m][0:2, :]
        for peer in peers:
            pltpu.make_async_remote_copy(
                msg.at[step], got.at[step, me], ssem.at[step], rsem.at[step],
                device_id={"tiles": peer}, device_id_type=MESH,
            ).start()
        pltpu.make_async_copy(msg.at[step], got.at[step, me], rsem.at[step]).start()
        if step == STEPS - 1:
            emsg[...] = (picked[0] + picked[1])[0:2, :]
            pl.semaphore_wait(all_in, ENS - 1)
            for stranger in strangers:
                pltpu.make_async_remote_copy(
                    emsg, egot.at[ye, me], esend, erecv, device_id=stranger, device_id_type=MESH
                ).start()

    places = []

    def slot_sums(values, m):
        for j in range(LAKE_DEV // 4):
            leaves = [
                total_of([jnp.where(at == float(p), v, 0.0) for at, v in zip(places, values)])
                for p in range(4 * j, 4 * j + 4)
            ]
            lines[m, j * 8:j * 8 + 8, :] = merge4(leaves, lane, 32)

    def cascade(held, m, v):
        lateral = total_of([lines[m, pl.ds(v * 64 + r, 8, stride=8), :] for r in range(8)])
        full = held + lateral * (1.0 / 256.0)
        out = par[1, v] * full
        above = total_of([chain[k, v] * pltpu.roll(out, k + 1, 1) for k in range(DEPTH - 1)])
        out = out + par[1, v] * above
        return full + above - out, out

    def heard(step):
        pltpu.make_async_copy(got.at[step], got.at[step], rsem.at[step]).wait()
        places[:] = [pos[n] for n in range(TILES // 4)]
        return [
            [
                jnp.concatenate([got[step, 4 * n + d, m] for d in range(4)], axis=0)
                for n in range(TILES // 4)
            ]
            for m in range(MEMB)
        ]

    def hear(step):
        values = heard(step)
        for m in range(MEMB):
            slot_sums(values[m], m)
        for m in range(MEMB):
            for v in range(2):
                pool[m, v], out = cascade(pool[m, v], m, v)
                if step < STEPS - 1:
                    outf[m, v] = outf[m, v] + out
        return values

    def share_copies():
        return [
            pltpu.make_async_remote_copy(
                share, shared.at[ye], psend, precv, device_id={"ens": other}, device_id_type=MESH
            )
            for other in others
        ]

    def share_start():
        for v in range(2):
            share[0, v] = pool[0, v] + pool[1, v]
            share[1, v] = outf[0, v] + outf[1, v]
        for copy in share_copies():
            copy.start()
        pltpu.make_async_copy(share, shared.at[ye], precv).start()

    for side in (0, 1):
        still_copies[side].start()
    for p in range(PARTS):
        for copy in halo_copies(0, p):
            copy.start()
    for m in range(MEMB):
        flows(0, m)

    pltpu.make_async_copy(greet, greet, isem).wait()
    for k in range(4):
        pick = (lane & 15) * 4 + k
        for b in range(4):
            tile = jnp.zeros((8, 128), F32)
            for kind in range(5):
                rows = greet[b * 8:b * 8 + 8, 2 + kind, :]
                tile = jnp.where((lane >> 4) == kind, lanes_of(rows, pick), tile)
            turn[k * 32 + b * 8:k * 32 + b * 8 + 8, :] = tile
    turn[...] = jnp.transpose(turn[...])
    links = []
    for v in range(2):
        used = sub + 8 * v < LAKE_DEV // 4
        rows = [turn[16 * kind + 8 * v:16 * kind + 8 * v + 8, :] for kind in range(5)]
        for m in range(MEMB):
            pool[m, v] = rows[m]
            outf[m, v] = jnp.zeros((8, 128), F32)
        par[0, v] = 1.0 / jnp.where(used, rows[2], 1.0)
        par[1, v] = rows[3]
        links.append(rows[4])

    def settle():
        for n in range(TILES // 4):
            pos[n] = jnp.concatenate([greet[4 * n + d, 0:2, :] for d in range(4)], axis=0)
        for m in range(MEMB + 1):
            lines[m, 80:128, :] = jnp.zeros((48, 128), F32)
        for v in range(2):
            factor, run = par[1, v] * links[v], links[v]
            for k in range(DEPTH - 1):
                chain[k, v] = run
                run = run * pltpu.roll(factor, k + 1, 1)

    for copy in still_copies:
        copy.wait_recv()
    for step in range(STEPS):
        edge_flows(step)
        if step > 0:
            hear(step - 1)
        sums = drain(step)
        tell(step, sums)
        if step == 0:
            settle()
        if step == STEPS - 1:
            share_start()
        else:
            for m in range(MEMB):
                flows(step + 1, m)
    values = hear(STEPS - 1)

    pltpu.make_async_copy(shared, shared, precv).wait()
    pltpu.make_async_copy(egot.at[1:], egot.at[1:], erecv).wait()
    everyone = []
    for n in range(TILES // 4):
        mine = values[0][n] + values[1][n]
        everyone.append(
            total_of(
                [
                    jnp.where(
                        ye == y,
                        mine,
                        jnp.concatenate([egot[y, 4 * n + d] for d in range(4)], axis=0),
                    )
                    for y in range(ENS)
                ]
            )
        )
    slot_sums(everyone, MEMB)
    sum_of = [
        [total_of([shared[y, kind, v] for y in range(ENS)]) for v in range(2)] for kind in range(2)
    ]
    outflow = [sum_of[1][v] + cascade(sum_of[0][v], MEMB, v)[1] for v in range(2)]

    pick = (lane & 3) * 32 + me
    own = [jnp.zeros((8, 128), F32) for _ in range(2)]
    for j in range(LAKE_DEV // 4):
        here = (lane >> 2) == j
        v, r = j // 8, j % 8
        for m in range(MEMB):
            own[0] = jnp.where(
                here & (sub == m), lanes_of(spread(pool[m, v, r:r + 1, :]), pick), own[0]
            )
        own[1] = jnp.where(here, lanes_of(spread(outflow[v][r:r + 1, :]), pick), own[1])
    new_storage[...] = own[0][0:2, 0:LAKE_DEV]
    ens_outflow[...] = (own[1] * (1.0 / (MEMB * ENS)))[0:1, 0:LAKE_DEV]

    pltpu.make_async_copy(greet.at[1:], greet.at[1:], psem).wait()
    for copy in still_copies:
        copy.wait_send()
    for step in range(STEPS):
        for p in range(PARTS):
            for copy in halo_copies(step, p):
                copy.wait_send()
        pltpu.make_async_copy(got.at[step, 1:], got.at[step, 1:], ssem.at[step]).wait()
    pltpu.make_async_copy(shared.at[1:], shared.at[1:], psend).wait()
    pltpu.make_async_copy(egot.at[1:], egot.at[1:], esend).wait()


def hand_out(water, pool, outflow, new_depth, new_storage, ens_outflow, sem):
    copies = [
        pltpu.make_async_copy(a, b, sem.at[n])
        for n, (a, b) in enumerate(
            [
                (water.at[0], new_depth.at[0]), (water.at[1], new_depth.at[1]),
                (pool, new_storage), (outflow, ens_outflow),
            ]
        )
    ]
    for copy in copies:
        copy.start()
    for copy in copies:
        copy.wait()


def shards(
    depth, bed, rain, rough_class, class_n, contact_seg, contact_lake, lake_slot,
    storage, area, release, upstream_link,
):
    far = pl.BlockSpec(memory_space=pltpu.HBM)
    vmem = pl.BlockSpec(memory_space=pltpu.VMEM)
    dma = pltpu.SemaphoreType.DMA
    results = pl.pallas_call(
        kernel,
        out_shape=(
            jax.ShapeDtypeStruct((MEMB, ROWS, COLS), F32),
            jax.ShapeDtypeStruct((MEMB, LAKE_DEV), F32),
            jax.ShapeDtypeStruct((1, LAKE_DEV), F32),
        ),
        in_specs=[far] * 12,
        out_specs=(vmem, vmem, vmem),
        scratch_shapes=[
            pltpu.VMEM((MEMB, ROWS, COLS), F32),
            pltpu.VMEM((MEMB, ROWS, COLS), F32),
            pltpu.VMEM((ROWS, COLS), F32),
            pltpu.VMEM((ROWS, COLS), F32),
            pltpu.VMEM((MEMB, ROWS, COLS + 128), F32),
            pltpu.VMEM((ROWS, COLS), I32),
            pltpu.SMEM((1, 8, TILES), I32),
            pltpu.SMEM((1, 8, TILES), I32),
            pltpu.SMEM((TILES * LAKE_DEV,), I32),
            pltpu.VMEM((1, 16), F32),
            pltpu.VMEM((MEMB, LAKE_DEV), F32),
            pltpu.VMEM((1, LAKE_DEV), F32),
            pltpu.VMEM((1, LAKE_DEV), F32),
            pltpu.VMEM((1, LAKE_DEV), I32),
            pltpu.VMEM((8, 128), F32),
            pltpu.VMEM((TILES, 8, 128), F32),
            pltpu.VMEM((128, 128), F32),
            pltpu.VMEM((TILES // 4, 8, 128), F32),
            pltpu.VMEM((MEMB, 2, 8, 128), F32),
            pltpu.VMEM((MEMB, 2, 8, 128), F32),
            pltpu.VMEM((2, 2, 8, 128), F32),
            pltpu.VMEM((DEPTH - 1, 2, 8, 128), F32),
            pltpu.VMEM((2, 2, BLOCKS, 8, 128), F32),
            pltpu.VMEM((2, 2, BLOCKS, 8, 128), F32),
            pltpu.VMEM((STEPS, 2, MEMB, BLOCKS, 8, 128), F32),
            pltpu.VMEM((STEPS, 2, MEMB, BLOCKS, 8, 128), F32),
            pltpu.VMEM((2, MEMB, BLOCKS, 8, 128), F32),
            pltpu.VMEM((MEMB, BLOCKS + 1, 8, 8, 128), F32),
            pltpu.VMEM((MEMB, BLOCKS, 8, 8, 128), F32),
            pltpu.VMEM((MEMB + 1, 128, 128), F32),
            pltpu.VMEM((STEPS, MEMB, 2, 128), F32),
            pltpu.VMEM((STEPS, TILES, MEMB, 2, 128), F32),
            pltpu.VMEM((2, 128), F32),
            pltpu.VMEM((ENS, TILES, 2, 128), F32),
            pltpu.VMEM((2, 2, 8, 128), F32),
            pltpu.VMEM((ENS, 2, 2, 8, 128), F32),
            dma((12,)),
            dma,
            dma,
            dma((STEPS,)),
            dma((STEPS,)),
            dma((STEPS, 2, PARTS)),
            dma((STEPS, 2, PARTS)),
            dma((2,)),
            dma((2,)),
            dma,
            dma,
            dma,
            dma,
            pltpu.SemaphoreType.REGULAR,
        ],
        compiler_params=pltpu.CompilerParams(
            collective_id=0, has_side_effects=True, vmem_limit_bytes=40 * 1024 * 1024
        ),
    )(
        *[
            pltpu.with_memory_space_constraint(a, pltpu.HBM)
            for a in (
                depth, bed, rain, rough_class, class_n.reshape(1, -1),
                contact_seg.transpose(0, 2, 1), contact_lake.transpose(0, 2, 1),
                lake_slot, storage, area.reshape(1, -1), release.reshape(1, -1),
                upstream_link.reshape(1, -1),
            )
        ]
    )
    water, pool, outflow = pl.pallas_call(
        hand_out,
        out_shape=[jax.ShapeDtypeStruct(r.shape, r.dtype) for r in results],
        in_specs=[vmem] * 3,
        out_specs=(far, far, far),
        scratch_shapes=[dma((4,))],
        compiler_params=pltpu.CompilerParams(vmem_limit_bytes=1024 * 1024),
    )(*results)
    return water, pool, outflow.reshape(-1)


def solution(mesh):
    return jax.shard_map(
        shards,
        mesh=mesh,
        in_specs=(
            P("ens", "tiles", None),
            P("tiles", None),
            P("ens", "tiles", None),
            P("tiles", None),
            P(),
            P("tiles", None, None),
            P("tiles", None, None),
            P(),
            P("ens", "tiles"),
            P("tiles"),
            P("tiles"),
            P("tiles"),
        ),
        out_specs=(P("ens", "tiles", None), P("ens", "tiles"), P("tiles")),
        check_vma=False,
    )
```
